256 devices in a mesh: dp: 32 (over x, y, core), tensor: 8 (over z).
Axes of the slice: x: 4, y: 4, z: 8, core: 2. Of those that a mesh axis runs over, the one named last changes fastest.
Arguments:
- user_feats: bfloat16 [32768, 1024], P(('dp', 'tensor')), may hold values from -240 to 240
- item_feats: bfloat16 [32768, 1024], P(('dp', 'tensor')), may hold values from -6 to 6
- user_w_in: bfloat16 [1024, 8192], P(None, 'tensor'), may hold values from -0.1875 to 0.1875
- user_w_out: bfloat16 [8192, 1024], P('tensor'), may hold values from -0.0625 to 0.0625
- item_w_in: bfloat16 [1024, 8192], P(None, 'tensor'), may hold values from -0.1875 to 0.1875
- item_w_out: bfloat16 [8192, 1024], P('tensor'), may hold values from -0.0625 to 0.0625
- teacher: float32 [32768, 2048], P(('dp', 'tensor')), may hold values from -250 to 250
- cand_blocks: int32 [256, 16], P(('dp', 'tensor')), may hold values from 0 to 31, all different within a row
- cand_count: int32 [256], P(('dp', 'tensor')), may hold values from 10 to 16
- owner_map: int32 [32], replicated, may hold values from 0 to 31, each once
Outputs:
- divergence: float32 [32768], P(('dp', 'tensor'))
- user_grad: float32 [32768, 1024], P(('dp', 'tensor'))
- item_grad: float32 [32768, 1024], P(('dp', 'tensor'))
The draws below stay inside these ranges and needn't reach their ends.
Inputs may be any that keep to these rules, and one draw needn't show every extreme that they name: `cand_blocks`: the 16 ids of one row are distinct. `owner_map`: every dp index appears exactly once.
All inputs are finite; a program needn't handle non-finite values.
Results may differ from the reference program's by a relative error of at most 0.017.
The reference program's roundings to bfloat16 on the way count: a program that leaves them out, or rounds other values in their place, can miss the bound.
Values may be sent and summed in bfloat16 or wider, within the bound.
A program may use at most 128 MiB of HBM per device.

```python
import math
import jax
import jax.numpy as jnp
from jax import lax

D = 1024
FF = 8192
BLK = 128
K = 16
USERS = 32768
ITEMS = 32768
N_DP = 32
N_TENSOR = 8


def draw_user_feats(key, part):
    values = jnp.clip(jax.random.normal(key, (USERS, D), jnp.float32), -6.0, 6.0)
    return values.astype(jnp.bfloat16)


def draw_teacher(key, part):
    return jnp.clip(3.0 * jax.random.normal(key, (USERS, K * BLK), jnp.float32), -15.0, 15.0)


def plant(drawn, stream_key, low, largest):
    place = [jax.random.randint(jax.random.fold_in(stream_key, axis), (), 0, length) for axis, length in enumerate(drawn.shape)]
    longest = drawn.shape.index(max(drawn.shape))
    next_to = place[:longest] + [(place[longest] + 1) % drawn.shape[longest]] + place[longest + 1:]
    return drawn.at[tuple(place)].set(low).at[tuple(next_to)].set(largest)


def shard_levels(rng, extent, shards, least, largest):
    def one(axis_at, parts):
        draws = jax.random.uniform(jax.random.fold_in(jax.random.fold_in(rng, 6), axis_at), (parts,), jnp.float32, least / len(shards), largest / len(shards))
        return jnp.repeat(jnp.exp(draws), extent[axis_at] // parts).reshape((-1,) + (1,) * (len(extent) - axis_at - 1))

    factor_of = one(*shards[0])
    for cut in shards[1:]:
        factor_of = factor_of * one(*cut)
    return factor_of


def different_ones(stream_key, rows, amount, top, lift):
    order = jax.random.permutation(jax.random.fold_in(stream_key, 1), amount)
    favour = order
    for power in range(3):
        favour = favour * favour // amount
    favour = favour * lift // amount
    lots = jax.random.randint(jax.random.fold_in(stream_key, 2), (rows, amount), 0, 4096) + favour
    holders = jax.random.permutation(jax.random.fold_in(stream_key, 3), rows)[jnp.arange(amount) % rows]
    lots = jnp.where(jnp.arange(rows)[:, None] == holders[None, :], 1 << 14, lots)
    merit = lots * amount + jnp.arange(amount)
    return lax.top_k(merit.astype(jnp.int32), top)[1].astype(jnp.int32)


def bell_draw(stream_key, dims, spread, most, shards=(), held_as=jnp.bfloat16):
    factor_of = shard_levels(stream_key, dims, shards, -0.22, 0.18) if shards else 1.0
    entries = jax.random.normal(stream_key, dims, jnp.float32) * spread * factor_of
    return jnp.minimum(jnp.maximum(entries, -most), most).astype(held_as)


def setup_inputs(seed: int = 0) -> dict:
    splits = jax.random.split(jax.random.key(seed), 11)
    return {
        "user_feats": draw_user_feats(jax.random.fold_in(splits[10], 71), 0),
        "item_feats": bell_draw(splits[1], (ITEMS, D), 1.0, 6.0, ((0, 256),)),
        "user_w_in": bell_draw(splits[2], (D, FF), D ** -0.5, 0.1875, ((1, 8),)),
        "user_w_out": bell_draw(splits[3], (FF, D), FF ** -0.5, 0.0625, ((0, 8),)),
        "item_w_in": bell_draw(splits[4], (D, FF), D ** -0.5, 0.1875, ((1, 8),)),
        "item_w_out": bell_draw(splits[5], (FF, D), FF ** -0.5, 0.0625, ((0, 8),)),
        "teacher": draw_teacher(jax.random.fold_in(splits[10], 71), 0),
        "cand_blocks": different_ones(splits[7], (N_DP * N_TENSOR), N_DP, K, 8192),
        "cand_count": plant(jax.random.randint(splits[8], (N_DP * N_TENSOR,), 5 * K // 8, K + 1), jax.random.fold_in(splits[8], 1), 5 * K // 8, K).astype(jnp.int32),
        "owner_map": jax.random.permutation(splits[9], N_DP).astype(jnp.int32),
    }


def tower_apply(feats, w_in, w_out):

    def one_group(row_group):
        hidden = jax.nn.relu(jnp.dot(row_group, w_in, preferred_element_type=jnp.float32)).astype(jnp.bfloat16)
        return jnp.dot(hidden, w_out, preferred_element_type=jnp.float32).astype(jnp.bfloat16)
    grouped = feats.reshape(-1, BLK * N_TENSOR, feats.shape[1])
    return lax.map(one_group, grouped).reshape(feats.shape[0], w_out.shape[1])

def masked_softmax(logits, usable):
    highest = lax.optimization_barrier(jnp.max(jnp.where(usable, logits, -jnp.inf), axis=(1, 2), keepdims=True))
    shifted = jnp.where(usable, logits - highest, -jnp.inf)
    exponent = jnp.exp(shifted)
    denominator = lax.optimization_barrier(jnp.sum(exponent, axis=(1, 2), keepdims=True))
    log_prob = jnp.where(usable, shifted - jnp.log(denominator), 0.0)
    return (exponent / denominator, log_prob)

def reference(user_feats, item_feats, user_w_in, user_w_out, item_w_in, item_w_out, teacher, cand_blocks, cand_count, owner_map):
    user_emb = tower_apply(user_feats, user_w_in, user_w_out)
    item_emb = tower_apply(item_feats, item_w_in, item_w_out)
    item_blocks = item_emb.reshape(N_DP * N_TENSOR, BLK, D)
    user_blocks = user_emb.reshape(N_DP * N_TENSOR, BLK, D)
    teacher_blocks = teacher.reshape(N_DP * N_TENSOR, BLK, K, BLK)
    logit_scale = 3.0 / math.sqrt(D)
    loss_weight = BLK * K / 4.0

    def per_block(item_sums, scanned):
        block_index, user_rows, teacher_rows, candidates, live_count = scanned
        tensor_index = block_index % N_TENSOR
        targets = (owner_map[candidates] * N_TENSOR + tensor_index).astype(jnp.int32)
        picked = item_blocks[targets]
        student = logit_scale * jnp.einsum('ud,kjd->ukj', user_rows.astype(jnp.float32), picked.astype(jnp.float32))
        usable = (jnp.arange(K) < live_count)[None, :, None]
        teacher_prob, log_teacher = masked_softmax(teacher_rows, usable)
        student_prob, log_student = masked_softmax(student, usable)
        divergence = lax.optimization_barrier(jnp.sum(jnp.where(usable, teacher_prob * (log_teacher - log_student), 0.0), axis=(1, 2)))
        logit_grads = (loss_weight * logit_scale * (student_prob - teacher_prob)).astype(jnp.bfloat16)
        user_grad = jnp.einsum('ukj,kjd->ud', logit_grads.astype(jnp.float32), picked.astype(jnp.float32))
        contrib = jnp.einsum('ukj,ud->kjd', logit_grads.astype(jnp.float32), user_rows.astype(jnp.float32)).astype(jnp.bfloat16)
        item_sums = item_sums.at[targets].add(contrib.astype(jnp.float32))
        return (item_sums, (divergence, user_grad))
    start_sums = jnp.zeros((N_DP * N_TENSOR, BLK, D), jnp.float32)
    scanned = (jnp.arange(N_DP * N_TENSOR, dtype=jnp.int32), user_blocks, teacher_blocks, cand_blocks, cand_count)
    item_sums, (divergence, user_grad) = lax.scan(per_block, start_sums, scanned)
    return (divergence.reshape(-1), user_grad.reshape(-1, D), item_sums.reshape(-1, D))
```

```python
import functools
import math

import jax
import jax.numpy as jnp
from jax import lax
from jax.experimental import pallas as pl
from jax.experimental.pallas import tpu as pltpu
from jax.sharding import PartitionSpec as P

BLK = 128
D = 1024
SLOTS = 16
OWNERS = 32
SIDE = 4
OFF = (0, 3, 1, 2)
F32 = jnp.float32
BF16 = jnp.bfloat16


def dp_copy(src, dst, send_sem, recv_sem, target):
    return pltpu.make_async_remote_copy(
        src_ref=src,
        dst_ref=dst,
        send_sem=send_sem,
        recv_sem=recv_sem,
        device_id={"dp": target},
        device_id_type=pl.DeviceIdType.MESH,
    )


class PlaneGather:
    def __init__(self, table, send, recv):
        self.table, self.send, self.recv = table, send, recv
        me = lax.axis_index("dp")
        core = lax.rem(me, 2)
        x, y = me // 8, lax.rem(me // 2, SIDE)
        self.me, self.core = me, core
        self.a = x + core * (y - x)
        self.b = y + core * (x - y)
        self.stride_a = SIDE - 3 * core
        self.stride_b = 1 + 3 * core
        self.pending = []

    def index(self, off_a, off_b):
        a = lax.rem(self.a + off_a, SIDE)
        b = lax.rem(self.b + off_b, SIDE)
        return (a * self.stride_a + b * self.stride_b) * 2 + self.core

    def partner_index(self, off_a, off_b):
        other = 1 - self.core
        a = lax.rem(self.b + off_a, SIDE)
        b = lax.rem(self.a + off_b, SIDE)
        return (a * self.stride_b + b * self.stride_a) * 2 + other

    def block(self, slot, half=None):
        if half is None:
            return self.table.at[slot]
        return self.table.at[slot, pl.ds(half * (BLK // 2), BLK // 2)]

    def go(self, ident, slot, target, half=None):
        ref = self.block(slot, half)
        copy = dp_copy(ref, ref, self.send.at[ident], self.recv.at[ident], target)
        copy.start()
        self.pending.append(copy)

    def arrived(self, ident, slot, half=None):
        ref = self.block(slot, half)
        dp_copy(ref, ref, self.send.at[ident], self.recv.at[ident], self.me).wait_recv()

    def to_partner(self, qa, qb):
        self.go(20 + 4 * qa + qb, self.index(OFF[qa], OFF[qb]), self.me + 1 - 2 * self.core)

    def along_b(self, q):
        slot = self.index(OFF[q], 0)
        self.go(4 + 2 * q, slot, self.index(0, 1))
        self.go(5 + 2 * q, slot, self.index(0, 3))

    def start(self):
        slot = self.index(0, 0)
        self.go(0, slot, self.index(1, 0))
        self.go(1, slot, self.index(3, 0))
        self.along_b(0)
        self.to_partner(0, 0)

    def from_a(self, side):
        q = 1 + side
        slot = self.index(OFF[q], 0)
        self.arrived(side, slot)
        self.go(2 + side, slot, self.index(1 if side == 0 else 3, 0), side)
        self.along_b(q)
        self.to_partner(q, 0)

    def far_a(self):
        slot = self.index(2, 0)
        self.arrived(2, slot, 0)
        self.arrived(3, slot, 1)
        self.along_b(3)
        self.to_partner(3, 0)

    def from_b(self, q, side):
        slot = self.index(OFF[q], OFF[1 + side])
        self.arrived(4 + 2 * q + side, slot)
        self.go(12 + 2 * q + side, slot, self.index(0, 1 if side == 0 else 3), side)
        self.to_partner(q, 1 + side)

    def far_b(self, q):
        slot = self.index(OFF[q], 2)
        self.arrived(12 + 2 * q, slot, 0)
        self.arrived(13 + 2 * q, slot, 1)
        self.to_partner(q, 3)

    def from_partner(self, qa, qb):
        self.arrived(20 + 4 * qa + qb, self.partner_index(OFF[qa], OFF[qb]))

    def drain(self):
        for copy in self.pending:
            copy.wait_send()

    def relay_events(self):
        both = ((0,), (1,))
        return (
            [functools.partial(self.from_a, s) for (s,) in both]
            + [functools.partial(self.from_b, 0, s) for (s,) in both]
            + [self.far_a]
            + [functools.partial(self.from_b, 1, s) for (s,) in both]
            + [functools.partial(self.from_b, 2, s) for (s,) in both]
            + [functools.partial(self.far_b, 0)]
            + [functools.partial(self.from_b, 3, s) for (s,) in both]
        )

    def last_events(self):
        return [functools.partial(self.far_b, q) for q in (1, 2, 3)]

    def partner_events(self):
        return [functools.partial(self.from_partner, qa, qb) for qa in range(4) for qb in range(4)]


def dp_kernel(
    owned_ref,
    teacher_ref,
    cand_ref,
    count_ref,
    owner_ref,
    div_ref,
    user_grad_ref,
    item_grad_ref,
    items,
    users,
    logits,
    grads,
    grads_t,
    g_send,
    g_recv,
    pos_ref,
    inv_ref,
    i_send,
    i_recv,
    u_send,
    u_recv,
    x_send,
    x_recv,
):
    me = lax.axis_index("dp")
    barrier = pltpu.get_barrier_semaphore()

    def greet(i, carry):
        pl.semaphore_signal(
            barrier,
            inc=1,
            device_id={"dp": lax.rem(me + i, OWNERS)},
            device_id_type=pl.DeviceIdType.MESH,
        )
        return carry

    lax.fori_loop(1, OWNERS, greet, 0)
    items[me] = owned_ref[pl.ds(BLK, BLK), :].astype(BF16)
    users[me] = owned_ref[pl.ds(0, BLK), :].astype(BF16)
    pl.semaphore_wait(barrier, OWNERS - 1)

    item_gather = PlaneGather(items, i_send, i_recv)
    user_gather = PlaneGather(users, u_send, u_recv)
    item_gather.start()

    live = count_ref[0]
    scale = 3.0 / math.sqrt(D)
    weight = BLK * SLOTS / 4.0 * scale

    def place(k, carry):
        pos_ref[k] = owner_ref[cand_ref[0, k]]
        return carry

    lax.fori_loop(0, SLOTS, place, 0)

    def invert(j, carry):
        found = jnp.int32(SLOTS)
        for k in range(SLOTS):
            found = jnp.where((pos_ref[k] == j) & (k < live), k, found)
        inv_ref[j] = found
        return carry

    lax.fori_loop(0, OWNERS, invert, 0)

    def teacher_block(k):
        return teacher_ref[:, pl.ds(pl.multiple_of(k * BLK, BLK), BLK)]

    def usable(k, value, other):
        return jnp.where(k < live, value, other)

    def row_max(block):
        def step(k, high):
            return jnp.maximum(high, usable(k, block(k), -jnp.inf))

        high = lax.fori_loop(0, SLOTS, step, jnp.full((BLK, BLK), -jnp.inf, F32))
        return jnp.max(high, axis=1, keepdims=True)

    def row_sum(block, high):
        def step(k, total):
            return total + usable(k, jnp.exp(block(k) - high), 0.0)

        total = lax.fori_loop(0, SLOTS, step, jnp.zeros((BLK, BLK), F32))
        return jnp.sum(total, axis=1, keepdims=True)

    teacher_high = row_max(teacher_block)
    teacher_sum = row_sum(teacher_block, teacher_high)
    teacher_log = jnp.log(teacher_sum)

    for event in item_gather.relay_events():
        event()
    user_gather.start()
    for event in item_gather.last_events():
        event()
    user_events = user_gather.relay_events()
    for event in user_events[:2]:
        event()
    for event in item_gather.partner_events():
        event()

    def logit_step(k, carry):
        picked = items[pos_ref[k]]
        logits[k] = scale * lax.dot_general(
            users[me], picked, (((1,), (1,)), ((), ())), preferred_element_type=F32
        )
        return carry

    for part in range(4):
        lax.fori_loop(4 * part, 4 * part + 4, logit_step, 0)
        user_events[2 + part]()

    def student_block(k):
        return logits[k]

    student_high = row_max(student_block)
    student_sum = row_sum(student_block, student_high)
    student_log = jnp.log(student_sum)
    user_events[6]()
    user_events[7]()

    def grad_step(k, total):
        t_shift = teacher_block(k) - teacher_high
        s_shift = student_block(k) - student_high
        p = jnp.exp(t_shift) / teacher_sum
        q = jnp.exp(s_shift) / student_sum
        gap = (t_shift - teacher_log) - (s_shift - student_log)
        g = usable(k, weight * (q - p), 0.0)
        grads[k] = g.astype(BF16)
        grads_t[k] = g.T.astype(BF16)
        return total + usable(k, p * gap, 0.0)

    total = jnp.zeros((BLK, BLK), F32)
    for part in range(2):
        total = lax.fori_loop(8 * part, 8 * part + 8, grad_step, total)
        user_events[8 + part]()
    grads_t[SLOTS] = jnp.zeros((BLK, BLK), BF16)

    def exchange(slot, target):
        return dp_copy(
            g_send.at[target], g_recv.at[slot], x_send.at[target], x_recv.at[slot], target
        )

    def send_grads(i, carry):
        target = lax.rem(me + i, OWNERS)
        g_send[target] = grads_t[inv_ref[target]]
        exchange(me, target).start()
        return carry

    lax.fori_loop(1, OWNERS, send_grads, 0)
    g_recv[me] = grads_t[inv_ref[me]]

    for event in user_events[10:]:
        event()
    for event in user_gather.last_events():
        event()

    row_total = jnp.broadcast_to(jnp.sum(total, axis=1, keepdims=True), (BLK, BLK))
    div_ref[...] = row_total.T[0:1, :]

    wide = 256
    for chunk in range(D // wide):
        cols = pl.ds(chunk * wide, wide)

        def user_step(k, acc):
            return acc + jnp.dot(grads[k], items[pos_ref[k], :, cols], preferred_element_type=F32)

        user_grad_ref[:, cols] = lax.fori_loop(0, SLOTS, user_step, jnp.zeros((BLK, wide), F32))

    for event in user_gather.partner_events():
        event()

    def landed(i, carry):
        source = lax.rem(me + OWNERS - i, OWNERS)
        dp_copy(
            g_send.at[source], g_recv.at[source], x_send.at[source], x_recv.at[source], me
        ).wait_recv()
        return carry

    lax.fori_loop(1, OWNERS, landed, 0)

    for chunk in range(D // wide):
        cols = pl.ds(chunk * wide, wide)

        def item_step(j, acc):
            contrib = jnp.dot(g_recv[j], users[j, :, cols], preferred_element_type=F32)
            return acc + contrib.astype(BF16).astype(F32)

        item_grad_ref[:, cols] = lax.fori_loop(0, OWNERS, item_step, jnp.zeros((BLK, wide), F32))

    item_gather.drain()
    user_gather.drain()

    def drained(i, carry):
        target = lax.rem(me + i, OWNERS)
        exchange(me, target).wait_send()
        return carry

    lax.fori_loop(1, OWNERS, drained, 0)


def dp_phase(owned, teacher, cand, count, owner_map):
    vmem = pl.BlockSpec(memory_space=pltpu.VMEM)
    smem = pl.BlockSpec(memory_space=pltpu.SMEM)
    return pl.pallas_call(
        dp_kernel,
        out_shape=(
            jax.ShapeDtypeStruct((1, BLK), F32),
            jax.ShapeDtypeStruct((BLK, D), F32),
            jax.ShapeDtypeStruct((BLK, D), F32),
        ),
        in_specs=[vmem, vmem, smem, smem, smem],
        out_specs=(vmem, vmem, vmem),
        scratch_shapes=[
            pltpu.VMEM((OWNERS, BLK, D), BF16),
            pltpu.VMEM((OWNERS, BLK, D), BF16),
            pltpu.VMEM((SLOTS, BLK, BLK), F32),
            pltpu.VMEM((SLOTS, BLK, BLK), BF16),
            pltpu.VMEM((SLOTS + 1, BLK, BLK), BF16),
            pltpu.VMEM((OWNERS, BLK, BLK), BF16),
            pltpu.VMEM((OWNERS, BLK, BLK), BF16),
            pltpu.SMEM((SLOTS,), jnp.int32),
            pltpu.SMEM((OWNERS,), jnp.int32),
            pltpu.SemaphoreType.DMA((36,)),
            pltpu.SemaphoreType.DMA((36,)),
            pltpu.SemaphoreType.DMA((36,)),
            pltpu.SemaphoreType.DMA((36,)),
            pltpu.SemaphoreType.DMA((OWNERS,)),
            pltpu.SemaphoreType.DMA((OWNERS,)),
        ],
        compiler_params=pltpu.CompilerParams(
            collective_id=0, has_side_effects=True, vmem_limit_bytes=48 * 1024 * 1024
        ),
        name="dp_phase",
    )(owned, teacher, cand, count, owner_map)


def shards(
    user_feats,
    item_feats,
    user_w_in,
    user_w_out,
    item_w_in,
    item_w_out,
    teacher,
    cand_blocks,
    cand_count,
    owner_map,
):
    both = jnp.concatenate((user_feats, item_feats), axis=1)
    gathered = lax.all_gather(both, "tensor", axis=0, tiled=True)

    def tower(feats, w_in, w_out):
        hidden = jax.nn.relu(jnp.dot(feats, w_in, preferred_element_type=F32)).astype(BF16)
        return jnp.dot(hidden, w_out, preferred_element_type=F32)

    user_out = tower(gathered[:, :D], user_w_in, user_w_out)
    item_out = tower(gathered[:, D:], item_w_in, item_w_out)
    stacked = jnp.stack((user_out.reshape(-1, BLK, D), item_out.reshape(-1, BLK, D)), axis=1)
    owned = lax.psum_scatter(
        stacked.reshape(2 * BLK * lax.axis_size("tensor"), D),
        "tensor",
        scatter_dimension=0,
        tiled=True,
    )
    divergence, user_grad, item_grad = dp_phase(owned, teacher, cand_blocks, cand_count, owner_map)
    return (divergence.reshape(BLK), user_grad, item_grad)


def solution(mesh):
    placed = (
        P(("dp", "tensor"), None),
        P(("dp", "tensor"), None),
        P(None, "tensor"),
        P("tensor", None),
        P(None, "tensor"),
        P("tensor", None),
        P(("dp", "tensor"), None),
        P(("dp", "tensor"), None),
        P(("dp", "tensor")),
        P(),
    )
    return jax.shard_map(
        shards,
        mesh=mesh,
        in_specs=placed,
        out_specs=(P(("dp", "tensor")), P(("dp", "tensor"), None), P(("dp", "tensor"), None)),
        check_vma=False,
    )
```

```python
import functools
import math

import jax
import jax.numpy as jnp
from jax import lax
from jax.experimental import pallas as pl
from jax.experimental.pallas import tpu as pltpu
from jax.sharding import PartitionSpec as P

BLK = 128
D = 1024
SLOTS = 16
OWNERS = 32
SIDE = 4
OFF = (0, 3, 1, 2)
SHARE = BLK // SIDE
RING = 8
FAR2, FAR1, NEAR, OWN = range(4)
F32 = jnp.float32
BF16 = jnp.bfloat16


def dp_copy(src, dst, send_sem, recv_sem, target):
    return pltpu.make_async_remote_copy(
        src_ref=src,
        dst_ref=dst,
        send_sem=send_sem,
        recv_sem=recv_sem,
        device_id={"dp": target},
        device_id_type=pl.DeviceIdType.MESH,
    )


def z_copy(src, dst, send_sem, recv_sem, target):
    return pltpu.make_async_remote_copy(
        src_ref=src,
        dst_ref=dst,
        send_sem=send_sem,
        recv_sem=recv_sem,
        device_id={"tensor": target},
        device_id_type=pl.DeviceIdType.MESH,
    )


class PlaneGather:
    def __init__(self, table, send, recv):
        self.table, self.send, self.recv = table, send, recv
        self.half_rows = table.shape[1] // 2
        me = lax.axis_index("dp")
        core = lax.rem(me, 2)
        x, y = me // 8, lax.rem(me // 2, SIDE)
        self.me, self.core = me, core
        self.a = x + core * (y - x)
        self.b = y + core * (x - y)
        self.stride_a = SIDE - 3 * core
        self.stride_b = 1 + 3 * core
        self.pending = []

    def index(self, off_a, off_b):
        a = lax.rem(self.a + off_a, SIDE)
        b = lax.rem(self.b + off_b, SIDE)
        return (a * self.stride_a + b * self.stride_b) * 2 + self.core

    def partner_index(self, off_a, off_b):
        other = 1 - self.core
        a = lax.rem(self.b + off_a, SIDE)
        b = lax.rem(self.a + off_b, SIDE)
        return (a * self.stride_b + b * self.stride_a) * 2 + other

    def block(self, slot, half=None):
        if half is None:
            return self.table.at[slot]
        return self.table.at[slot, pl.ds(half * self.half_rows, self.half_rows)]

    def go(self, ident, slot, target, half=None):
        ref = self.block(slot, half)
        copy = dp_copy(ref, ref, self.send.at[ident], self.recv.at[ident], target)
        copy.start()
        self.pending.append(copy)

    def arrived(self, ident, slot, half=None):
        ref = self.block(slot, half)
        dp_copy(ref, ref, self.send.at[ident], self.recv.at[ident], self.me).wait_recv()

    def to_partner(self, qa, qb):
        self.go(20 + 4 * qa + qb, self.index(OFF[qa], OFF[qb]), self.me + 1 - 2 * self.core)

    def along_b(self, q):
        slot = self.index(OFF[q], 0)
        self.go(4 + 2 * q, slot, self.index(0, 1))
        self.go(5 + 2 * q, slot, self.index(0, 3))

    def start(self):
        slot = self.index(0, 0)
        self.go(0, slot, self.index(1, 0))
        self.go(1, slot, self.index(3, 0))
        self.along_b(0)
        self.to_partner(0, 0)

    def from_a(self, side):
        q = 1 + side
        slot = self.index(OFF[q], 0)
        self.arrived(side, slot)
        self.go(2 + side, slot, self.index(1 if side == 0 else 3, 0), side)
        self.along_b(q)
        self.to_partner(q, 0)

    def far_a(self):
        slot = self.index(2, 0)
        self.arrived(2, slot, 0)
        self.arrived(3, slot, 1)
        self.along_b(3)
        self.to_partner(3, 0)

    def from_b(self, q, side):
        slot = self.index(OFF[q], OFF[1 + side])
        self.arrived(4 + 2 * q + side, slot)
        self.go(12 + 2 * q + side, slot, self.index(0, 1 if side == 0 else 3), side)
        self.to_partner(q, 1 + side)

    def far_b(self, q):
        slot = self.index(OFF[q], 2)
        self.arrived(12 + 2 * q, slot, 0)
        self.arrived(13 + 2 * q, slot, 1)
        self.to_partner(q, 3)

    def from_partner(self, qa, qb):
        self.arrived(20 + 4 * qa + qb, self.partner_index(OFF[qa], OFF[qb]))

    def drain(self):
        for copy in self.pending:
            copy.wait_send()

    def relay_events(self):
        both = ((0,), (1,))
        return (
            [functools.partial(self.from_a, s) for (s,) in both]
            + [functools.partial(self.from_b, 0, s) for (s,) in both]
            + [self.far_a]
            + [functools.partial(self.from_b, 1, s) for (s,) in both]
            + [functools.partial(self.from_b, 2, s) for (s,) in both]
            + [functools.partial(self.far_b, 0)]
            + [functools.partial(self.from_b, 3, s) for (s,) in both]
        )

    def last_events(self):
        return [functools.partial(self.far_b, q) for q in (1, 2, 3)]

    def partner_events(self):
        return [functools.partial(self.from_partner, qa, qb) for qa in range(4) for qb in range(4)]


class Tower:
    def __init__(self, feats, shard, hidden, partial, returned, table, sems):
        self.feats, self.shard, self.hidden = feats, shard, hidden
        self.partial, self.returned, self.table = partial, returned, table
        self.send, self.recv = sems
        self.z = lax.axis_index("tensor")
        self.me = lax.axis_index("dp")
        self.sign = 1 - 2 * lax.rem(self.me, 2)
        self.pending = []

    def at(self, steps):
        return lax.rem(self.z + steps * self.sign + RING, RING)

    def go(self, ident, src, dst, target):
        copy = z_copy(src, dst, self.send.at[ident], self.recv.at[ident], target)
        copy.start()
        self.pending.append(copy)

    def arrived(self, ident, dst):
        z_copy(dst, dst, self.send.at[ident], self.recv.at[ident], self.z).wait_recv()

    def rows(self, slot):
        return self.feats.at[pl.ds(slot * BLK, BLK)]

    def send_features(self):
        self.go(0, self.shard, self.rows(FAR1), self.at(1))
        self.go(1, self.shard, self.rows(NEAR), self.at(-1))

    def pass_features(self):
        self.arrived(0, self.rows(FAR1))
        self.go(2, self.rows(FAR1), self.rows(FAR2), self.at(1))

    def features_here(self):
        self.arrived(1, self.rows(NEAR))
        self.arrived(2, self.rows(FAR2))

    def gemm(self, pair, w_in, w_out, more):
        rows = pl.ds(pair * 2 * BLK, 2 * BLK)
        wide = 256

        def into_hidden(n, carry):
            cols = pl.ds(pl.multiple_of(n * wide, wide), wide)
            out = jnp.dot(self.feats[rows, :], w_in(cols), preferred_element_type=F32)
            self.hidden[:, cols] = jnp.maximum(out, 0.0).astype(BF16)
            return carry

        def into_partial(n, carry):
            cols = pl.ds(pl.multiple_of(n * wide, wide), wide)
            out = jnp.dot(self.hidden[...], w_out(cols), preferred_element_type=F32)
            if more:
                out = out + self.partial[rows, cols]
            self.partial[rows, cols] = out
            return carry

        lax.fori_loop(0, D // wide, into_hidden, 0)
        lax.fori_loop(0, D // wide, into_partial, 0)

    def half(self, ref, slot, part):
        return ref.at[pl.ds(slot * BLK + part * (BLK // 2), BLK // 2)]

    def send_far(self):
        for part in range(2):
            self.go(
                3 + part,
                self.half(self.partial, FAR2, part),
                self.half(self.returned, 0, part),
                self.at(-1),
            )

    def send_near(self):
        self.go(7, self.rows_of(self.partial, NEAR), self.rows_of(self.returned, 2), self.at(1))

    def rows_of(self, ref, slot):
        return ref.at[pl.ds(slot * BLK, BLK)]

    def pass_far(self, part):
        self.arrived(3 + part, self.half(self.returned, 0, part))
        mine = pl.ds(FAR1 * BLK + part * (BLK // 2), BLK // 2)
        self.partial[mine, :] = self.partial[mine, :] + self.returned[pl.ds(part * (BLK // 2), BLK // 2), :]
        self.go(
            5 + part,
            self.half(self.partial, FAR1, part),
            self.half(self.returned, 1, part),
            self.at(-1),
        )

    def finish(self):
        for part in range(2):
            self.arrived(5 + part, self.half(self.returned, 1, part))
        self.arrived(7, self.rows_of(self.returned, 2))
        total = self.partial[pl.ds(OWN * BLK, BLK), :] + self.returned[pl.ds(BLK, BLK), :]
        self.table[self.me] = (total + self.returned[pl.ds(2 * BLK, BLK), :]).astype(BF16)

    def drain(self):
        for copy in self.pending:
            copy.wait_send()


def step_kernel(
    user_feats,
    item_feats,
    user_w_in,
    user_w_out,
    item_w_in,
    item_w_out,
    teacher_hbm,
    cand_ref,
    count_ref,
    owner_ref,
    div_ref,
    user_grad_ref,
    item_grad_ref,
    items,
    users,
    own_w,
    item_w,
    user_w,
    item_rows,
    user_rows,
    hidden,
    item_partial,
    user_partial,
    item_returned,
    user_returned,
    teacher_ref,
    logits,
    grads,
    grads_t,
    g_send,
    g_recv,
    pos_ref,
    inv_ref,
    load_sem,
    shift_send,
    shift_recv,
    zi_send,
    zi_recv,
    zu_send,
    zu_recv,
    plane_send,
    plane_recv,
    x_send,
    x_recv,
):
    me = lax.axis_index("dp")
    z = lax.axis_index("tensor")
    opposite = lax.rem(z + RING // 2, RING)
    barrier = pltpu.get_barrier_semaphore()

    def greet(i, carry):
        pl.semaphore_signal(
            barrier,
            inc=1,
            device_id={"dp": lax.rem(me + i, OWNERS)},
            device_id_type=pl.DeviceIdType.MESH,
        )
        return carry

    lax.fori_loop(1, OWNERS, greet, 0)
    for steps in (1, RING // 2, RING - 1):
        pl.semaphore_signal(
            barrier,
            inc=1,
            device_id={"tensor": lax.rem(z + steps, RING)},
            device_id_type=pl.DeviceIdType.MESH,
        )

    last = pl.ds(OWN * BLK, BLK)
    loads = [
        pltpu.make_async_copy(item_feats, item_rows.at[last], load_sem.at[0]),
        pltpu.make_async_copy(item_w_in, own_w.at[0], load_sem.at[1]),
        pltpu.make_async_copy(item_w_out, own_w.at[1], load_sem.at[2]),
        pltpu.make_async_copy(user_feats, user_rows.at[last], load_sem.at[3]),
        pltpu.make_async_copy(user_w_in, own_w.at[2], load_sem.at[4]),
        pltpu.make_async_copy(user_w_out, own_w.at[3], load_sem.at[5]),
        pltpu.make_async_copy(teacher_hbm, teacher_ref, load_sem.at[6]),
    ]
    for load in loads:
        load.start()

    live = count_ref[0]

    def place(k, carry):
        pos_ref[k] = owner_ref[cand_ref[0, k]]
        return carry

    lax.fori_loop(0, SLOTS, place, 0)

    pl.semaphore_wait(barrier, OWNERS - 1 + 3)

    item_tower = Tower(
        item_rows, item_feats, hidden, item_partial, item_returned, items, (zi_send, zi_recv)
    )
    user_tower = Tower(
        user_rows, user_feats, hidden, user_partial, user_returned, users, (zu_send, zu_recv)
    )
    gathers = [
        PlaneGather(table, plane_send.at[n], plane_recv.at[n])
        for n, table in enumerate((item_w, user_w, items, users))
    ]
    item_w_gather, user_w_gather, item_gather, user_gather = gathers
    share = pl.ds(pl.multiple_of(me * SHARE, SHARE), SHARE)

    def shift(n):
        table = (item_w, item_w, user_w, user_w)[n]
        ref = (item_w_in, item_w_out, user_w_in, user_w_out)[n]
        return z_copy(
            ref.at[share],
            table.at[me, pl.ds((n % 2) * SHARE, SHARE)],
            shift_send.at[n],
            shift_recv.at[n],
            opposite,
        )

    for n in (0, 1):
        shift(n).start()
    item_tower.send_features()
    user_tower.send_features()
    for n in (2, 3):
        shift(n).start()

    def own_weights(n):
        return lambda cols: own_w[n, :, cols]

    def far_weights(table, part):
        def pick(cols):
            return table[:, pl.ds(part * SHARE, SHARE), cols].reshape(D, cols.size)

        return pick

    item_own = (own_weights(0), own_weights(1))
    user_own = (own_weights(2), own_weights(3))
    item_far = (far_weights(item_w, 0), far_weights(item_w, 1))
    user_far = (far_weights(user_w, 0), far_weights(user_w, 1))

    def run(events):
        for event in events:
            event()

    for n in (0, 1):
        shift(n).wait_recv()
    item_w_gather.start()
    item_tower.pass_features()
    events = item_w_gather.relay_events()
    run(events[:2])
    user_tower.pass_features()
    run(events[2:4])
    for load in loads[:3]:
        load.wait()
    item_tower.features_here()
    run(events[4:5])
    item_tower.gemm(0, *item_own, False)
    run(events[5:7])
    item_tower.gemm(1, *item_own, False)
    run(events[7:9])
    for load in loads[3:]:
        load.wait()
    user_tower.features_here()
    run(events[9:])
    for n in (2, 3):
        shift(n).wait_recv()
    user_w_gather.start()
    user_tower.gemm(0, *user_own, False)
    run(item_w_gather.last_events())
    events = user_w_gather.relay_events()
    run(events[:2])
    user_tower.gemm(1, *user_own, False)
    run(item_w_gather.partner_events())
    run(events[2:4])
    item_tower.gemm(0, *item_far, True)
    item_tower.send_far()
    run(events[4:7])
    item_tower.gemm(1, *item_far, True)
    item_tower.send_near()
    run(events[7:])
    run(user_w_gather.last_events())
    item_tower.pass_far(0)
    item_tower.pass_far(1)
    run(user_w_gather.partner_events())
    user_tower.gemm(0, *user_far, True)
    user_tower.send_far()
    user_tower.gemm(1, *user_far, True)
    user_tower.send_near()

    def invert(j, carry):
        found = jnp.int32(SLOTS)
        for k in range(SLOTS):
            found = jnp.where((pos_ref[k] == j) & (k < live), k, found)
        inv_ref[j] = found
        return carry

    lax.fori_loop(0, OWNERS, invert, 0)

    scale = 3.0 / math.sqrt(D)
    weight = BLK * SLOTS / 4.0 * scale

    def teacher_block(k):
        return teacher_ref[:, pl.ds(pl.multiple_of(k * BLK, BLK), BLK)]

    def usable(k, value, other):
        return jnp.where(k < live, value, other)

    def row_max(block):
        def step(k, high):
            return jnp.maximum(high, usable(k, block(k), -jnp.inf))

        high = lax.fori_loop(0, SLOTS, step, jnp.full((BLK, BLK), -jnp.inf, F32))
        return jnp.max(high, axis=1, keepdims=True)

    def row_sum(block, high):
        def step(k, total):
            return total + usable(k, jnp.exp(block(k) - high), 0.0)

        total = lax.fori_loop(0, SLOTS, step, jnp.zeros((BLK, BLK), F32))
        return jnp.sum(total, axis=1, keepdims=True)

    teacher_high = row_max(teacher_block)
    teacher_sum = row_sum(teacher_block, teacher_high)
    teacher_log = jnp.log(teacher_sum)

    item_tower.finish()
    item_gather.start()
    events = item_gather.relay_events()
    run(events[:4])
    user_tower.pass_far(0)
    user_tower.pass_far(1)
    run(events[4:])
    user_tower.finish()
    user_gather.start()
    run(item_gather.last_events())
    user_events = user_gather.relay_events()
    run(user_events[:2])
    run(item_gather.partner_events())

    def logit_step(k, carry):
        picked = items[pos_ref[k]]
        logits[k] = scale * lax.dot_general(
            users[me], picked, (((1,), (1,)), ((), ())), preferred_element_type=F32
        )
        return carry

    for part in range(4):
        lax.fori_loop(4 * part, 4 * part + 4, logit_step, 0)
        user_events[2 + part]()

    def student_block(k):
        return logits[k]

    student_high = row_max(student_block)
    student_sum = row_sum(student_block, student_high)
    student_log = jnp.log(student_sum)
    user_events[6]()
    user_events[7]()

    def grad_step(k, total):
        t_shift = teacher_block(k) - teacher_high
        s_shift = student_block(k) - student_high
        p = jnp.exp(t_shift) / teacher_sum
        q = jnp.exp(s_shift) / student_sum
        gap = (t_shift - teacher_log) - (s_shift - student_log)
        g = usable(k, weight * (q - p), 0.0)
        grads[k] = g.astype(BF16)
        grads_t[k] = g.T.astype(BF16)
        return total + usable(k, p * gap, 0.0)

    total = jnp.zeros((BLK, BLK), F32)
    for part in range(2):
        total = lax.fori_loop(8 * part, 8 * part + 8, grad_step, total)
        user_events[8 + part]()
    grads_t[SLOTS] = jnp.zeros((BLK, BLK), BF16)

    def exchange(slot, target):
        return dp_copy(
            g_send.at[target], g_recv.at[slot], x_send.at[target], x_recv.at[slot], target
        )

    def send_grads(i, carry):
        target = lax.rem(me + i, OWNERS)
        g_send[target] = grads_t[inv_ref[target]]
        exchange(me, target).start()
        return carry

    lax.fori_loop(1, OWNERS, send_grads, 0)
    g_recv[me] = grads_t[inv_ref[me]]

    run(user_events[10:])
    run(user_gather.last_events())

    row_total = jnp.broadcast_to(jnp.sum(total, axis=1, keepdims=True), (BLK, BLK))
    div_ref[...] = row_total.T[0:1, :]

    wide = 256
    for chunk in range(D // wide):
        cols = pl.ds(chunk * wide, wide)

        def user_step(k, acc):
            return acc + jnp.dot(grads[k], items[pos_ref[k], :, cols], preferred_element_type=F32)

        user_grad_ref[:, cols] = lax.fori_loop(0, SLOTS, user_step, jnp.zeros((BLK, wide), F32))

    run(user_gather.partner_events())

    def landed(i, carry):
        source = lax.rem(me + OWNERS - i, OWNERS)
        dp_copy(
            g_send.at[source], g_recv.at[source], x_send.at[source], x_recv.at[source], me
        ).wait_recv()
        return carry

    lax.fori_loop(1, OWNERS, landed, 0)

    for chunk in range(D // wide):
        cols = pl.ds(chunk * wide, wide)

        def item_step(j, acc):
            contrib = jnp.dot(g_recv[j], users[j, :, cols], preferred_element_type=F32)
            return acc + contrib.astype(BF16).astype(F32)

        item_grad_ref[:, cols] = lax.fori_loop(0, OWNERS, item_step, jnp.zeros((BLK, wide), F32))

    for n in range(4):
        shift(n).wait_send()
    item_tower.drain()
    user_tower.drain()
    for gather in gathers:
        gather.drain()

    def drained(i, carry):
        target = lax.rem(me + i, OWNERS)
        exchange(me, target).wait_send()
        return carry

    lax.fori_loop(1, OWNERS, drained, 0)


def shards(
    user_feats,
    item_feats,
    user_w_in,
    user_w_out,
    item_w_in,
    item_w_out,
    teacher,
    cand_blocks,
    cand_count,
    owner_map,
):
    hbm = pl.BlockSpec(memory_space=pl.ANY)
    vmem = pl.BlockSpec(memory_space=pltpu.VMEM)
    smem = pl.BlockSpec(memory_space=pltpu.SMEM)
    dma = pltpu.SemaphoreType.DMA
    divergence, user_grad, item_grad = pl.pallas_call(
        step_kernel,
        out_shape=(
            jax.ShapeDtypeStruct((1, BLK), F32),
            jax.ShapeDtypeStruct((BLK, D), F32),
            jax.ShapeDtypeStruct((BLK, D), F32),
        ),
        in_specs=[hbm] * 7 + [smem] * 3,
        out_specs=(vmem, vmem, vmem),
        scratch_shapes=[
            pltpu.VMEM((OWNERS, BLK, D), BF16),
            pltpu.VMEM((OWNERS, BLK, D), BF16),
            pltpu.VMEM((4, D, D), BF16),
            pltpu.VMEM((OWNERS, 2 * SHARE, D), BF16),
            pltpu.VMEM((OWNERS, 2 * SHARE, D), BF16),
            pltpu.VMEM((4 * BLK, D), BF16),
            pltpu.VMEM((4 * BLK, D), BF16),
            pltpu.VMEM((2 * BLK, D), BF16),
            pltpu.VMEM((4 * BLK, D), F32),
            pltpu.VMEM((4 * BLK, D), F32),
            pltpu.VMEM((3 * BLK, D), F32),
            pltpu.VMEM((3 * BLK, D), F32),
            pltpu.VMEM((BLK, SLOTS * BLK), F32),
            pltpu.VMEM((SLOTS, BLK, BLK), F32),
            pltpu.VMEM((SLOTS, BLK, BLK), BF16),
            pltpu.VMEM((SLOTS + 1, BLK, BLK), BF16),
            pltpu.VMEM((OWNERS, BLK, BLK), BF16),
            pltpu.VMEM((OWNERS, BLK, BLK), BF16),
            pltpu.SMEM((SLOTS,), jnp.int32),
            pltpu.SMEM((OWNERS,), jnp.int32),
            dma((7,)),
            dma((4,)),
            dma((4,)),
            dma((8,)),
            dma((8,)),
            dma((8,)),
            dma((8,)),
            dma((4, 36)),
            dma((4, 36)),
            dma((OWNERS,)),
            dma((OWNERS,)),
        ],
        compiler_params=pltpu.CompilerParams(
            collective_id=0, has_side_effects=True, vmem_limit_bytes=62 * 1024 * 1024
        ),
        name="distill_step",
    )(
        user_feats,
        item_feats,
        user_w_in,
        user_w_out,
        item_w_in,
        item_w_out,
        teacher,
        cand_blocks,
        cand_count,
        owner_map,
    )
    return (divergence.reshape(BLK), user_grad, item_grad)


def solution(mesh):
    placed = (
        P(("dp", "tensor"), None),
        P(("dp", "tensor"), None),
        P(None, "tensor"),
        P("tensor", None),
        P(None, "tensor"),
        P("tensor", None),
        P(("dp", "tensor"), None),
        P(("dp", "tensor"), None),
        P(("dp", "tensor")),
        P(),
    )
    return jax.shard_map(
        shards,
        mesh=mesh,
        in_specs=placed,
        out_specs=(P(("dp", "tensor")), P(("dp", "tensor"), None), P(("dp", "tensor"), None)),
        check_vma=False,
    )
```

```python
import functools
import math

import jax
import jax.numpy as jnp
from jax import lax
from jax.experimental import pallas as pl
from jax.experimental.pallas import tpu as pltpu
from jax.sharding import PartitionSpec as P

BLK = 128
D = 1024
SLOTS = 16
OWNERS = 32
SIDE = 4
OFF = (0, 3, 1, 2)
SHARE = BLK // SIDE
RING = 8
FAR2, FAR1, NEAR, OWN = range(4)
F32 = jnp.float32
BF16 = jnp.bfloat16


def dp_copy(src, dst, send_sem, recv_sem, target):
    return pltpu.make_async_remote_copy(
        src_ref=src,
        dst_ref=dst,
        send_sem=send_sem,
        recv_sem=recv_sem,
        device_id={"dp": target},
        device_id_type=pl.DeviceIdType.MESH,
    )


def z_copy(src, dst, send_sem, recv_sem, target):
    return pltpu.make_async_remote_copy(
        src_ref=src,
        dst_ref=dst,
        send_sem=send_sem,
        recv_sem=recv_sem,
        device_id={"tensor": target},
        device_id_type=pl.DeviceIdType.MESH,
    )


ORDER = (
    "shift_i", "tstat", "invert", "WI.start", "feats_i", "WI.from_a0", "WI.from_a1", "WI.from_b00",
    "WI.from_b01", "pass_i", "shift_u", "feats_u", "WI.far_a", "own1_i", "WI.from_b10", "WI.from_b11",
    "WI.from_b20", "WI.from_b21", "WI.far_b0", "WI.from_b30", "WI.from_b31", "WI.far_b1", "WI.far_b2",
    "WI.far_b3", "WI.partners", "own0_i", "far0_i", "sendfar_i", "far1_i", "sendnear_i", "pass_u", "own1_u",
    "WU.start", "pass0_i", "WU.from_a0", "WU.from_a1", "WU.from_b00", "WU.from_b01", "pass1_i", "WU.far_a",
    "WU.from_b10", "WU.from_b11", "WU.from_b20", "WU.from_b21", "WU.far_b0", "own0_u", "WU.far_b1",
    "WU.far_b2", "WU.from_b30", "WU.from_b31", "finish0_i", "IT0.start", "WU.far_b3", "finish1_i",
    "IT1.start", "WU.partners", "far0_u", "sendfar_u", "IT0.from_a0", "IT0.from_a1", "IT0.from_b00",
    "IT0.from_b01", "far1_u", "sendnear_u", "IT1.from_a0", "IT1.from_a1", "IT0.far_a", "IT1.from_b00",
    "IT0.from_b10", "IT0.from_b11", "IT1.from_b01", "pass0_u", "IT0.from_b21", "IT0.from_b20", "IT1.far_a",
    "IT0.far_b0", "IT1.from_b10", "IT1.from_b11", "IT1.from_b20", "IT1.from_b21", "pass1_u", "IT0.from_b30",
    "IT0.from_b31", "IT0.far_b1", "IT1.far_b0", "IT0.far_b2", "IT1.from_b30", "IT1.from_b31", "IT1.far_b1",
    "finish0_u", "IT1.far_b2", "US0.start", "IT0.far_b3", "IT1.far_b3", "IT0.partners", "IT1.partners",
    "finish1_u", "US1.start", "logit0", "logit1", "US0.from_a0", "US0.from_a1", "US0.from_b00",
    "US0.from_b01", "logit2", "logit3", "sstat", "US0.far_a", "US1.from_a0", "US0.from_b10", "US0.from_b11",
    "US1.from_a1", "US1.from_b00", "US1.from_b01", "grad0", "US0.from_b20", "US0.from_b21", "grad1", "a2a",
    "US0.far_b0", "US0.from_b30", "US0.from_b31", "US1.far_a", "US1.from_b10", "US1.from_b11", "ugrad",
    "US0.far_b1", "US1.from_b20", "US1.from_b21", "US1.far_b0", "US0.far_b2", "US0.far_b3", "US1.from_b30",
    "US1.from_b31", "US1.far_b1", "US1.far_b2", "landed", "own0", "US1.far_b3", "oth0", "own1", "oth1",
    "own2", "oth2", "own3", "oth3",
)


class PlaneGather:
    def __init__(self, table, base, rows, send, recv):
        self.table, self.base, self.rows = table, base, rows
        self.send, self.recv = send, recv
        me = lax.axis_index("dp")
        core = lax.rem(me, 2)
        x, y = me // 8, lax.rem(me // 2, SIDE)
        self.me, self.core = me, core
        self.a = x + core * (y - x)
        self.b = y + core * (x - y)
        self.stride_a = SIDE - 3 * core
        self.stride_b = 1 + 3 * core
        self.pending = []

    def index(self, off_a, off_b):
        a = lax.rem(self.a + off_a, SIDE)
        b = lax.rem(self.b + off_b, SIDE)
        return (a * self.stride_a + b * self.stride_b) * 2 + self.core

    def partner_index(self, off_a, off_b):
        other = 1 - self.core
        a = lax.rem(self.b + off_a, SIDE)
        b = lax.rem(self.a + off_b, SIDE)
        return (a * self.stride_b + b * self.stride_a) * 2 + other

    def block(self, slot, half=None):
        if half is None:
            return self.table.at[slot, pl.ds(self.base, self.rows)]
        return self.table.at[slot, pl.ds(self.base + half * (self.rows // 2), self.rows // 2)]

    def go(self, ident, slot, target, half=None):
        ref = self.block(slot, half)
        copy = dp_copy(ref, ref, self.send.at[ident], self.recv.at[ident], target)
        copy.start()
        self.pending.append(copy)

    def arrived(self, ident, slot, half=None):
        ref = self.block(slot, half)
        dp_copy(ref, ref, self.send.at[ident], self.recv.at[ident], self.me).wait_recv()

    def to_partner(self, qa, qb):
        self.go(20 + 4 * qa + qb, self.index(OFF[qa], OFF[qb]), self.me + 1 - 2 * self.core)

    def along_b(self, q):
        slot = self.index(OFF[q], 0)
        self.go(4 + 2 * q, slot, self.index(0, 1))
        self.go(5 + 2 * q, slot, self.index(0, 3))

    def start(self):
        slot = self.index(0, 0)
        self.go(0, slot, self.index(1, 0))
        self.go(1, slot, self.index(3, 0))
        self.along_b(0)
        self.to_partner(0, 0)

    def from_a(self, side):
        q = 1 + side
        slot = self.index(OFF[q], 0)
        self.arrived(side, slot)
        self.go(2 + side, slot, self.index(1 if side == 0 else 3, 0), side)
        self.along_b(q)
        self.to_partner(q, 0)

    def far_a(self):
        slot = self.index(2, 0)
        self.arrived(2, slot, 0)
        self.arrived(3, slot, 1)
        self.along_b(3)
        self.to_partner(3, 0)

    def from_b(self, q, side):
        slot = self.index(OFF[q], OFF[1 + side])
        self.arrived(4 + 2 * q + side, slot)
        self.go(12 + 2 * q + side, slot, self.index(0, 1 if side == 0 else 3), side)
        self.to_partner(q, 1 + side)

    def far_b(self, q):
        slot = self.index(OFF[q], 2)
        self.arrived(12 + 2 * q, slot, 0)
        self.arrived(13 + 2 * q, slot, 1)
        self.to_partner(q, 3)

    def from_partner(self, qa, qb):
        self.arrived(20 + 4 * qa + qb, self.partner_index(OFF[qa], OFF[qb]))

    def drain(self):
        for copy in self.pending:
            copy.wait_send()

    def partners(self):
        for qa in range(SIDE):
            for qb in range(SIDE):
                self.from_partner(qa, qb)

    def tasks(self, name):
        table = {
            name + ".start": self.start,
            name + ".far_a": self.far_a,
            name + ".partners": self.partners,
        }
        for side in range(2):
            table[name + ".from_a" + str(side)] = functools.partial(self.from_a, side)
        for q in range(SIDE):
            table[name + ".far_b" + str(q)] = functools.partial(self.far_b, q)
            for side in range(2):
                label = name + ".from_b" + str(q) + str(side)
                table[label] = functools.partial(self.from_b, q, side)
        return table


class Tower:
    def __init__(self, feats, shard, hidden, partial, returned, table, sems):
        self.feats, self.shard, self.hidden = feats, shard, hidden
        self.partial, self.returned, self.table = partial, returned, table
        self.send, self.recv = sems
        self.z = lax.axis_index("tensor")
        self.me = lax.axis_index("dp")
        self.sign = 1 - 2 * lax.rem(self.me, 2)
        self.pending = []

    def at(self, steps):
        return lax.rem(self.z + steps * self.sign + RING, RING)

    def go(self, ident, src, dst, target):
        copy = z_copy(src, dst, self.send.at[ident], self.recv.at[ident], target)
        copy.start()
        self.pending.append(copy)

    def arrived(self, ident, dst):
        z_copy(dst, dst, self.send.at[ident], self.recv.at[ident], self.z).wait_recv()

    def rows(self, slot):
        return self.feats.at[pl.ds(slot * BLK, BLK)]

    def send_features(self):
        self.go(0, self.shard, self.rows(FAR1), self.at(1))
        self.go(1, self.shard, self.rows(NEAR), self.at(-1))

    def pass_features(self):
        self.arrived(0, self.rows(FAR1))
        self.go(2, self.rows(FAR1), self.rows(FAR2), self.at(1))

    def features_here(self, pair):
        if pair == 0:
            self.arrived(2, self.rows(FAR2))
        else:
            self.arrived(1, self.rows(NEAR))

    def gemm(self, pair, w_in, w_out, more):
        rows = pl.ds(pair * 2 * BLK, 2 * BLK)
        wide = 256

        def into_hidden(n, carry):
            cols = pl.ds(pl.multiple_of(n * wide, wide), wide)
            out = jnp.dot(self.feats[rows, :], w_in(cols), preferred_element_type=F32)
            self.hidden[:, cols] = jnp.maximum(out, 0.0).astype(BF16)
            return carry

        def into_partial(n, carry):
            cols = pl.ds(pl.multiple_of(n * wide, wide), wide)
            out = jnp.dot(self.hidden[...], w_out(cols), preferred_element_type=F32)
            if more:
                out = out + self.partial[rows, cols]
            self.partial[rows, cols] = out
            return carry

        lax.fori_loop(0, D // wide, into_hidden, 0)
        lax.fori_loop(0, D // wide, into_partial, 0)

    def half(self, ref, slot, part):
        return ref.at[pl.ds(slot * BLK + part * (BLK // 2), BLK // 2)]

    def send_far(self):
        for part in range(2):
            self.go(
                3 + part,
                self.half(self.partial, FAR2, part),
                self.half(self.returned, 0, part),
                self.at(-1),
            )

    def send_near(self):
        for part in range(2):
            self.go(
                7 + part,
                self.half(self.partial, NEAR, part),
                self.half(self.returned, 2, part),
                self.at(1),
            )

    def pass_far(self, part):
        self.arrived(3 + part, self.half(self.returned, 0, part))
        mine = pl.ds(FAR1 * BLK + part * (BLK // 2), BLK // 2)
        self.partial[mine, :] = self.partial[mine, :] + self.returned[pl.ds(part * (BLK // 2), BLK // 2), :]
        self.go(
            5 + part,
            self.half(self.partial, FAR1, part),
            self.half(self.returned, 1, part),
            self.at(-1),
        )

    def finish(self, part):
        self.arrived(5 + part, self.half(self.returned, 1, part))
        self.arrived(7 + part, self.half(self.returned, 2, part))
        half = BLK // 2
        own, first, second = (
            pl.ds(slot * BLK + part * half, half) for slot in (OWN, 1, 2)
        )
        total = self.partial[own, :] + self.returned[first, :] + self.returned[second, :]
        self.table[self.me, pl.ds(part * half, half), :] = total.astype(BF16)

    def drain(self):
        for copy in self.pending:
            copy.wait_send()


def step_kernel(
    user_feats,
    item_feats,
    user_w_in,
    user_w_out,
    item_w_in,
    item_w_out,
    teacher_hbm,
    cand_ref,
    count_ref,
    owner_ref,
    div_ref,
    user_grad_ref,
    item_grad_ref,
    items,
    users,
    own_w,
    item_w,
    user_w,
    item_rows,
    user_rows,
    hidden,
    item_partial,
    user_partial,
    item_returned,
    user_returned,
    teacher_ref,
    logits,
    diverged,
    grads,
    grads_t,
    g_send,
    g_recv,
    pos_ref,
    inv_ref,
    load_sem,
    shift_send,
    shift_recv,
    zi_send,
    zi_recv,
    zu_send,
    zu_recv,
    plane_send,
    plane_recv,
    x_send,
    x_recv,
):
    me = lax.axis_index("dp")
    z = lax.axis_index("tensor")
    opposite = lax.rem(z + RING // 2, RING)
    barrier = pltpu.get_barrier_semaphore()

    def greet(i, carry):
        pl.semaphore_signal(
            barrier,
            inc=1,
            device_id={"dp": lax.rem(me + i, OWNERS)},
            device_id_type=pl.DeviceIdType.MESH,
        )
        return carry

    lax.fori_loop(1, OWNERS, greet, 0)
    for steps in (1, RING // 2, RING - 1):
        pl.semaphore_signal(
            barrier,
            inc=1,
            device_id={"tensor": lax.rem(z + steps, RING)},
            device_id_type=pl.DeviceIdType.MESH,
        )

    last = pl.ds(OWN * BLK, BLK)
    loads = [
        pltpu.make_async_copy(teacher_hbm, teacher_ref, load_sem.at[6]),
        pltpu.make_async_copy(item_feats, item_rows.at[last], load_sem.at[0]),
        pltpu.make_async_copy(item_w_in, own_w.at[0], load_sem.at[1]),
        pltpu.make_async_copy(item_w_out, own_w.at[1], load_sem.at[2]),
        pltpu.make_async_copy(user_feats, user_rows.at[last], load_sem.at[3]),
        pltpu.make_async_copy(user_w_in, own_w.at[2], load_sem.at[4]),
        pltpu.make_async_copy(user_w_out, own_w.at[3], load_sem.at[5]),
    ]
    for load in loads:
        load.start()

    live = count_ref[0]

    def place(k, carry):
        pos_ref[k] = owner_ref[cand_ref[0, k]]
        return carry

    lax.fori_loop(0, SLOTS, place, 0)

    pl.semaphore_wait(barrier, OWNERS - 1 + 3)

    item_tower = Tower(
        item_rows, item_feats, hidden, item_partial, item_returned, items, (zi_send, zi_recv)
    )
    user_tower = Tower(
        user_rows, user_feats, hidden, user_partial, user_returned, users, (zu_send, zu_recv)
    )
    pieces = (
        (item_w, 0, 2 * SHARE),
        (user_w, 0, 2 * SHARE),
        (items, 0, BLK // 2),
        (items, BLK // 2, BLK // 2),
        (users, 0, BLK // 2),
        (users, BLK // 2, BLK // 2),
    )
    gathers = [
        PlaneGather(*piece, plane_send.at[n], plane_recv.at[n]) for n, piece in enumerate(pieces)
    ]
    user_gathers = gathers[4:]
    share = pl.ds(pl.multiple_of(me * SHARE, SHARE), SHARE)

    def shift(n):
        table = (item_w, item_w, user_w, user_w)[n]
        ref = (item_w_in, item_w_out, user_w_in, user_w_out)[n]
        return z_copy(
            ref.at[share],
            table.at[me, pl.ds((n % 2) * SHARE, SHARE)],
            shift_send.at[n],
            shift_recv.at[n],
            opposite,
        )

    def own_weights(n):
        return lambda cols: own_w[n, :, cols]

    def far_weights(table, part):
        def pick(cols):
            return table[:, pl.ds(part * SHARE, SHARE), cols].reshape(D, cols.size)

        return pick

    item_own = (own_weights(0), own_weights(1))
    user_own = (own_weights(2), own_weights(3))
    item_far = (far_weights(item_w, 0), far_weights(item_w, 1))
    user_far = (far_weights(user_w, 0), far_weights(user_w, 1))

    def shift_start(first):
        for n in (first, first + 1):
            shift(n).start()

    def weights_start(gather, first):
        for n in (first, first + 1):
            shift(n).wait_recv()
        gather.start()

    def own_pair(tower, pair, weights, needed):
        if pair == 1:
            for load in needed:
                load.wait()
        tower.features_here(pair)
        tower.gemm(pair, *weights, False)

    def invert(j, carry):
        found = jnp.int32(SLOTS)
        for k in range(SLOTS):
            found = jnp.where((pos_ref[k] == j) & (k < live), k, found)
        inv_ref[j] = found
        return carry

    scale = 3.0 / math.sqrt(D)
    weight = BLK * SLOTS / 4.0 * scale

    def teacher_block(k):
        return teacher_ref[:, pl.ds(pl.multiple_of(k * BLK, BLK), BLK)]

    def usable(k, value, other):
        return jnp.where(k < live, value, other)

    def row_max(block):
        def step(k, high):
            return jnp.maximum(high, usable(k, block(k), -jnp.inf))

        high = lax.fori_loop(0, SLOTS, step, jnp.full((BLK, BLK), -jnp.inf, F32))
        return jnp.max(high, axis=1, keepdims=True)

    def row_sum(block, high):
        def step(k, total):
            return total + usable(k, jnp.exp(block(k) - high), 0.0)

        total = lax.fori_loop(0, SLOTS, step, jnp.zeros((BLK, BLK), F32))
        return jnp.sum(total, axis=1, keepdims=True)

    stats = {}

    def softmax_stats(name, block):
        high = row_max(block)
        total = row_sum(block, high)
        stats[name] = (high, total, jnp.log(total))

    def teacher_stats():
        loads[0].wait()
        softmax_stats("teacher", teacher_block)

    def logit_step(k, carry):
        picked = items[pos_ref[k]]
        logits[k] = scale * lax.dot_general(
            users[me], picked, (((1,), (1,)), ((), ())), preferred_element_type=F32
        )
        return carry

    def student_block(k):
        return logits[k]

    def gradients(part):
        teacher_high, teacher_sum, teacher_log = stats["teacher"]
        student_high, student_sum, student_log = stats["student"]

        def grad_step(k, total):
            t_shift = teacher_block(k) - teacher_high
            s_shift = student_block(k) - student_high
            p = jnp.exp(t_shift) / teacher_sum
            q = jnp.exp(s_shift) / student_sum
            gap = (t_shift - teacher_log) - (s_shift - student_log)
            g = usable(k, weight * (q - p), 0.0)
            grads[k] = g.astype(BF16)
            grads_t[k] = g.T.astype(BF16)
            return total + usable(k, p * gap, 0.0)

        before = jnp.zeros((BLK, BLK), F32) if part == 0 else diverged[...]
        half = SLOTS // 2
        diverged[...] = lax.fori_loop(half * part, half * part + half, grad_step, before)

    def exchange(slot, target):
        return dp_copy(
            g_send.at[target], g_recv.at[slot], x_send.at[target], x_recv.at[slot], target
        )

    def send_grads(i, carry):
        target = lax.rem(me + i, OWNERS)
        g_send[target] = grads_t[inv_ref[target]]
        exchange(me, target).start()
        return carry

    def all_to_all():
        grads_t[SLOTS] = jnp.zeros((BLK, BLK), BF16)
        lax.fori_loop(1, OWNERS, send_grads, 0)
        g_recv[me] = grads_t[inv_ref[me]]

    wide = 256

    def user_gradient():
        row_total = jnp.broadcast_to(jnp.sum(diverged[...], axis=1, keepdims=True), (BLK, BLK))
        div_ref[...] = row_total.T[0:1, :]
        for chunk in range(D // wide):
            cols = pl.ds(chunk * wide, wide)

            def user_step(k, acc):
                picked = items[pos_ref[k], :, cols]
                return acc + jnp.dot(grads[k], picked, preferred_element_type=F32)

            zero = jnp.zeros((BLK, wide), F32)
            user_grad_ref[:, cols] = lax.fori_loop(0, SLOTS, user_step, zero)

    def landed():
        def one(i, carry):
            source = lax.rem(me + OWNERS - i, OWNERS)
            dp_copy(
                g_send.at[source], g_recv.at[source], x_send.at[source], x_recv.at[source], me
            ).wait_recv()
            return carry

        lax.fori_loop(1, OWNERS, one, 0)

    written = []

    def item_gradient(sources):
        def one(n, carry):
            cols = pl.ds(pl.multiple_of(n * wide, wide), wide)
            acc = item_grad_ref[:, cols] if first_done else jnp.zeros((BLK, wide), F32)
            for j in sources:
                contrib = jnp.dot(g_recv[j], users[j, :, cols], preferred_element_type=F32)
                acc = acc + contrib.astype(BF16).astype(F32)
            item_grad_ref[:, cols] = acc
            return carry

        first_done = bool(written)
        written.append(True)
        lax.fori_loop(0, D // wide, one, 0)

    def from_own(qb):
        item_gradient([gathers[4].index(OFF[q], OFF[qb]) for q in range(SIDE)])

    def from_other(qb):
        for gather in user_gathers:
            for qa in range(SIDE):
                gather.from_partner(qa, qb)
        item_gradient([gathers[4].partner_index(OFF[q], OFF[qb]) for q in range(SIDE)])

    part = functools.partial
    tasks = {
        "invert": lambda: lax.fori_loop(0, OWNERS, invert, 0),
        "tstat": teacher_stats,
        "sstat": part(softmax_stats, "student", student_block),
        "a2a": all_to_all,
        "ugrad": user_gradient,
        "landed": landed,
    }
    for name, gather in zip(("WI", "WU", "IT0", "IT1", "US0", "US1"), gathers):
        tasks.update(gather.tasks(name))
    towers = (
        ("_i", item_tower, item_own, item_far, loads[1:4], gathers[0]),
        ("_u", user_tower, user_own, user_far, loads[4:7], gathers[1]),
    )
    for n, (end, tower, own, far, needed, gather) in enumerate(towers):
        tasks["shift" + end] = part(shift_start, 2 * n)
        tasks[("WI.start", "WU.start")[n]] = part(weights_start, gather, 2 * n)
        tasks["feats" + end] = tower.send_features
        tasks["pass" + end] = tower.pass_features
        for pair in range(2):
            tasks["own" + str(pair) + end] = part(own_pair, tower, pair, own, needed)
            tasks["far" + str(pair) + end] = part(tower.gemm, pair, *far, True)
            tasks["pass" + str(pair) + end] = part(tower.pass_far, pair)
            tasks["finish" + str(pair) + end] = part(tower.finish, pair)
        tasks["sendfar" + end] = tower.send_far
        tasks["sendnear" + end] = tower.send_near
    for n in range(4):
        tasks["logit" + str(n)] = part(lax.fori_loop, 4 * n, 4 * n + 4, logit_step, 0)
        tasks["own" + str(n)] = part(from_own, n)
        tasks["oth" + str(n)] = part(from_other, n)
    for n in range(2):
        tasks["grad" + str(n)] = part(gradients, n)
    for name in ORDER:
        tasks[name]()

    for n in range(4):
        shift(n).wait_send()
    item_tower.drain()
    user_tower.drain()
    for gather in gathers:
        gather.drain()

    def drained(i, carry):
        target = lax.rem(me + i, OWNERS)
        exchange(me, target).wait_send()
        return carry

    lax.fori_loop(1, OWNERS, drained, 0)


def shards(
    user_feats,
    item_feats,
    user_w_in,
    user_w_out,
    item_w_in,
    item_w_out,
    teacher,
    cand_blocks,
    cand_count,
    owner_map,
):
    hbm = pl.BlockSpec(memory_space=pl.ANY)
    vmem = pl.BlockSpec(memory_space=pltpu.VMEM)
    smem = pl.BlockSpec(memory_space=pltpu.SMEM)
    dma = pltpu.SemaphoreType.DMA
    divergence, user_grad, item_grad = pl.pallas_call(
        step_kernel,
        out_shape=(
            jax.ShapeDtypeStruct((1, BLK), F32),
            jax.ShapeDtypeStruct((BLK, D), F32),
            jax.ShapeDtypeStruct((BLK, D), F32),
        ),
        in_specs=[hbm] * 7 + [smem] * 3,
        out_specs=(vmem, vmem, vmem),
        scratch_shapes=[
            pltpu.VMEM((OWNERS, BLK, D), BF16),
            pltpu.VMEM((OWNERS, BLK, D), BF16),
            pltpu.VMEM((4, D, D), BF16),
            pltpu.VMEM((OWNERS, 2 * SHARE, D), BF16),
            pltpu.VMEM((OWNERS, 2 * SHARE, D), BF16),
            pltpu.VMEM((4 * BLK, D), BF16),
            pltpu.VMEM((4 * BLK, D), BF16),
            pltpu.VMEM((2 * BLK, D), BF16),
            pltpu.VMEM((4 * BLK, D), F32),
            pltpu.VMEM((4 * BLK, D), F32),
            pltpu.VMEM((3 * BLK, D), F32),
            pltpu.VMEM((3 * BLK, D), F32),
            pltpu.VMEM((BLK, SLOTS * BLK), F32),
            pltpu.VMEM((SLOTS, BLK, BLK), F32),
            pltpu.VMEM((BLK, BLK), F32),
            pltpu.VMEM((SLOTS, BLK, BLK), BF16),
            pltpu.VMEM((SLOTS + 1, BLK, BLK), BF16),
            pltpu.VMEM((OWNERS, BLK, BLK), BF16),
            pltpu.VMEM((OWNERS, BLK, BLK), BF16),
            pltpu.SMEM((SLOTS,), jnp.int32),
            pltpu.SMEM((OWNERS,), jnp.int32),
            dma((7,)),
            dma((4,)),
            dma((4,)),
            dma((9,)),
            dma((9,)),
            dma((9,)),
            dma((9,)),
            dma((6, 36)),
            dma((6, 36)),
            dma((OWNERS,)),
            dma((OWNERS,)),
        ],
        compiler_params=pltpu.CompilerParams(
            collective_id=0, has_side_effects=True, vmem_limit_bytes=62 * 1024 * 1024
        ),
        name="distill_step",
    )(
        user_feats,
        item_feats,
        user_w_in,
        user_w_out,
        item_w_in,
        item_w_out,
        teacher,
        cand_blocks,
        cand_count,
        owner_map,
    )
    return (divergence.reshape(BLK), user_grad, item_grad)


def solution(mesh):
    placed = (
        P(("dp", "tensor"), None),
        P(("dp", "tensor"), None),
        P(None, "tensor"),
        P("tensor", None),
        P(None, "tensor"),
        P("tensor", None),
        P(("dp", "tensor"), None),
        P(("dp", "tensor"), None),
        P(("dp", "tensor")),
        P(),
    )
    return jax.shard_map(
        shards,
        mesh=mesh,
        in_specs=placed,
        out_specs=(P(("dp", "tensor")), P(("dp", "tensor"), None), P(("dp", "tensor"), None)),
        check_vma=False,
    )
```

```python
import functools
import math

import jax
import jax.numpy as jnp
from jax import lax
from jax.experimental import pallas as pl
from jax.experimental.pallas import tpu as pltpu
from jax.sharding import PartitionSpec as P

BLK = 128
D = 1024
SLOTS = 16
OWNERS = 32
SIDE = 4
OFF = (0, 3, 1, 2)
SHARE = BLK // SIDE
RING = 8
FAR2, FAR1, NEAR, OWN = range(4)
F32 = jnp.float32
BF16 = jnp.bfloat16


def dp_copy(src, dst, send_sem, recv_sem, target):
    return pltpu.make_async_remote_copy(
        src_ref=src,
        dst_ref=dst,
        send_sem=send_sem,
        recv_sem=recv_sem,
        device_id={"dp": target},
        device_id_type=pl.DeviceIdType.MESH,
    )


def z_copy(src, dst, send_sem, recv_sem, target):
    return pltpu.make_async_remote_copy(
        src_ref=src,
        dst_ref=dst,
        send_sem=send_sem,
        recv_sem=recv_sem,
        device_id={"tensor": target},
        device_id_type=pl.DeviceIdType.MESH,
    )


ORDER = (
    "shift_i", "shift_u", "tstat", "invert", "WI.start", "feats_i", "WI.from_a0", "WI.from_a1", "WI.from_b00",
    "WI.from_b01", "WI.far_a", "WI.from_b10", "WI.from_b11", "WI.from_b20", "pass_i", "WI.from_b21",
    "WU.start", "feats_u", "WI.far_b0", "WI.from_b30", "WI.from_b31", "WI.far_b1", "WI.far_b2", "WU.from_a0",
    "WU.from_a1", "WU.from_b00", "WU.from_b01", "own_i", "pass_u", "WI.far_b3", "WU.far_a", "WU.from_b10",
    "WU.from_b11", "WU.from_b20", "WU.from_b21", "WU.far_b0", "WI.partners", "far0_i", "sendfar_i",
    "WU.far_b1", "WU.from_b30", "WU.from_b31", "far1_i", "WU.far_b2", "WU.far_b3", "own_u", "pass0_i",
    "sendnear_i", "pass1_i", "WU.partners", "far0_u", "sendfar_u", "far1_u", "sendnear_u", "finish0_i",
    "IT0.start", "IT0.from_a0", "IT0.from_a1", "IT0.from_b00", "IT0.from_b01", "finish1_i", "IT1.start",
    "IT0.far_a", "IT0.from_b11", "IT0.from_b10", "pass0_u", "IT1.from_a0", "IT1.from_a1", "IT0.from_b20",
    "IT0.from_b21", "IT0.far_b0", "IT1.far_a", "IT1.from_b00", "IT1.from_b01", "IT0.from_b30", "IT0.from_b31",
    "pass1_u", "IT0.far_b1", "IT1.from_b10", "IT1.from_b11", "IT1.from_b20", "finish0_u", "IT1.from_b21",
    "IT0.far_b2", "IT1.from_b30", "IT1.from_b31", "US0.start", "IT1.far_b0", "finish1_u", "US1.start",
    "IT0.far_b3", "IT1.far_b1", "IT0.partners", "IT1.far_b2", "US0.from_a0", "IT1.far_b3", "US0.from_a1",
    "IT1.partners", "logit0", "logit1", "logit2", "logit3", "sstat", "grad0", "grad1", "a2a", "US0.far_a",
    "US0.from_b00", "US0.from_b01", "US0.from_b10", "US0.from_b11", "US0.from_b20", "US0.from_b21",
    "US1.from_a0", "US1.from_a1", "US1.from_b00", "US1.from_b01", "ugrad", "US1.far_a", "US0.from_b30",
    "US0.from_b31", "US0.far_b0", "US0.far_b1", "US0.far_b2", "US1.from_b10", "US1.from_b11", "landed",
    "own0", "US1.from_b20", "US1.from_b21", "US1.far_b0", "oth0", "US1.from_b30", "US1.from_b31", "own1",
    "US0.far_b3", "oth1", "US1.far_b1", "US1.far_b2", "own2", "US1.far_b3", "oth2", "own3", "oth3",
)


class PlaneGather:
    def __init__(self, table, base, rows, send, recv):
        self.table, self.base, self.rows = table, base, rows
        self.send, self.recv = send, recv
        me = lax.axis_index("dp")
        core = lax.rem(me, 2)
        x, y = me // 8, lax.rem(me // 2, SIDE)
        self.me, self.core = me, core
        self.a = x + core * (y - x)
        self.b = y + core * (x - y)
        self.stride_a = SIDE - 3 * core
        self.stride_b = 1 + 3 * core
        self.pending = []

    def index(self, off_a, off_b):
        a = lax.rem(self.a + off_a, SIDE)
        b = lax.rem(self.b + off_b, SIDE)
        return (a * self.stride_a + b * self.stride_b) * 2 + self.core

    def partner_index(self, off_a, off_b):
        other = 1 - self.core
        a = lax.rem(self.b + off_a, SIDE)
        b = lax.rem(self.a + off_b, SIDE)
        return (a * self.stride_b + b * self.stride_a) * 2 + other

    def block(self, slot, half=None):
        if half is None:
            return self.table.at[slot, pl.ds(self.base, self.rows)]
        return self.table.at[slot, pl.ds(self.base + half * (self.rows // 2), self.rows // 2)]

    def go(self, ident, slot, target, half=None):
        ref = self.block(slot, half)
        copy = dp_copy(ref, ref, self.send.at[ident], self.recv.at[ident], target)
        copy.start()
        self.pending.append(copy)

    def arrived(self, ident, slot, half=None):
        ref = self.block(slot, half)
        dp_copy(ref, ref, self.send.at[ident], self.recv.at[ident], self.me).wait_recv()

    def to_partner(self, qa, qb):
        self.go(20 + 4 * qa + qb, self.index(OFF[qa], OFF[qb]), self.me + 1 - 2 * self.core)

    def along_b(self, q):
        slot = self.index(OFF[q], 0)
        self.go(4 + 2 * q, slot, self.index(0, 1))
        self.go(5 + 2 * q, slot, self.index(0, 3))

    def start(self):
        slot = self.index(0, 0)
        self.go(0, slot, self.index(1, 0))
        self.go(1, slot, self.index(3, 0))
        self.along_b(0)
        self.to_partner(0, 0)

    def from_a(self, side):
        q = 1 + side
        slot = self.index(OFF[q], 0)
        self.arrived(side, slot)
        self.go(2 + side, slot, self.index(1 if side == 0 else 3, 0), side)
        self.along_b(q)
        self.to_partner(q, 0)

    def far_a(self):
        slot = self.index(2, 0)
        self.arrived(2, slot, 0)
        self.arrived(3, slot, 1)
        self.along_b(3)
        self.to_partner(3, 0)

    def from_b(self, q, side):
        slot = self.index(OFF[q], OFF[1 + side])
        self.arrived(4 + 2 * q + side, slot)
        self.go(12 + 2 * q + side, slot, self.index(0, 1 if side == 0 else 3), side)
        self.to_partner(q, 1 + side)

    def far_b(self, q):
        slot = self.index(OFF[q], 2)
        self.arrived(12 + 2 * q, slot, 0)
        self.arrived(13 + 2 * q, slot, 1)
        self.to_partner(q, 3)

    def from_partner(self, qa, qb):
        self.arrived(20 + 4 * qa + qb, self.partner_index(OFF[qa], OFF[qb]))

    def drain(self):
        for copy in self.pending:
            copy.wait_send()

    def partners(self):
        for qa in range(SIDE):
            for qb in range(SIDE):
                self.from_partner(qa, qb)

    def tasks(self, name):
        table = {
            name + ".start": self.start,
            name + ".far_a": self.far_a,
            name + ".partners": self.partners,
        }
        for side in range(2):
            table[name + ".from_a" + str(side)] = functools.partial(self.from_a, side)
        for q in range(SIDE):
            table[name + ".far_b" + str(q)] = functools.partial(self.far_b, q)
            for side in range(2):
                label = name + ".from_b" + str(q) + str(side)
                table[label] = functools.partial(self.from_b, q, side)
        return table


class Tower:
    def __init__(self, feats, shard, hidden, partial, returned, table, sems):
        self.feats, self.shard, self.hidden = feats, shard, hidden
        self.partial, self.returned, self.table = partial, returned, table
        self.send, self.recv = sems
        self.z = lax.axis_index("tensor")
        self.me = lax.axis_index("dp")
        self.sign = 1 - 2 * lax.rem(self.me, 2)
        self.pending = []

    def at(self, steps):
        return lax.rem(self.z + steps * self.sign + RING, RING)

    def go(self, ident, src, dst, target):
        copy = z_copy(src, dst, self.send.at[ident], self.recv.at[ident], target)
        copy.start()
        self.pending.append(copy)

    def arrived(self, ident, dst):
        z_copy(dst, dst, self.send.at[ident], self.recv.at[ident], self.z).wait_recv()

    def rows(self, slot):
        return self.feats.at[pl.ds(slot * BLK, BLK)]

    def send_features(self):
        self.go(0, self.shard, self.rows(FAR1), self.at(1))
        self.go(1, self.shard, self.rows(NEAR), self.at(-1))

    def pass_features(self):
        self.arrived(0, self.rows(FAR1))
        self.go(2, self.rows(FAR1), self.rows(FAR2), self.at(1))

    def features_here(self):
        self.arrived(1, self.rows(NEAR))
        self.arrived(2, self.rows(FAR2))

    def gemm(self, first, count, w_in, w_out, more):
        rows = pl.ds(first * BLK, count * BLK)
        held = pl.ds(0, count * BLK)
        wide = 256

        def into_hidden(n, carry):
            cols = pl.ds(pl.multiple_of(n * wide, wide), wide)
            out = jnp.dot(self.feats[rows, :], w_in(cols), preferred_element_type=F32)
            self.hidden[held, cols] = jnp.maximum(out, 0.0).astype(BF16)
            return carry

        def into_partial(n, carry):
            cols = pl.ds(pl.multiple_of(n * wide, wide), wide)
            out = jnp.dot(self.hidden[held, :], w_out(cols), preferred_element_type=F32)
            if more:
                out = out + self.partial[rows, cols]
            self.partial[rows, cols] = out
            return carry

        lax.fori_loop(0, D // wide, into_hidden, 0)
        lax.fori_loop(0, D // wide, into_partial, 0)

    def half(self, ref, slot, part):
        return ref.at[pl.ds(slot * BLK + part * (BLK // 2), BLK // 2)]

    def send_far(self):
        for part in range(2):
            self.go(
                3 + part,
                self.half(self.partial, FAR2, part),
                self.half(self.returned, 0, part),
                self.at(-1),
            )

    def send_near(self):
        for part in range(2):
            self.go(
                7 + part,
                self.half(self.partial, NEAR, part),
                self.half(self.returned, 2, part),
                self.at(1),
            )

    def pass_far(self, part):
        self.arrived(3 + part, self.half(self.returned, 0, part))
        mine = pl.ds(FAR1 * BLK + part * (BLK // 2), BLK // 2)
        self.partial[mine, :] = self.partial[mine, :] + self.returned[pl.ds(part * (BLK // 2), BLK // 2), :]
        self.go(
            5 + part,
            self.half(self.partial, FAR1, part),
            self.half(self.returned, 1, part),
            self.at(-1),
        )

    def finish(self, part):
        self.arrived(5 + part, self.half(self.returned, 1, part))
        self.arrived(7 + part, self.half(self.returned, 2, part))
        half = BLK // 2
        own, first, second = (
            pl.ds(slot * BLK + part * half, half) for slot in (OWN, 1, 2)
        )
        total = self.partial[own, :] + self.returned[first, :] + self.returned[second, :]
        self.table[self.me, pl.ds(part * half, half), :] = total.astype(BF16)

    def drain(self):
        for copy in self.pending:
            copy.wait_send()


def step_kernel(
    user_feats,
    item_feats,
    user_w_in,
    user_w_out,
    item_w_in,
    item_w_out,
    teacher_hbm,
    cand_ref,
    count_ref,
    owner_ref,
    out_ref,
    items,
    users,
    own_w,
    item_w,
    user_w,
    item_rows,
    user_rows,
    hidden,
    item_partial,
    user_partial,
    item_returned,
    user_returned,
    teacher_ref,
    logits,
    diverged,
    grads,
    grads_t,
    g_send,
    g_recv,
    pos_ref,
    inv_ref,
    load_sem,
    shift_send,
    shift_recv,
    zi_send,
    zi_recv,
    zu_send,
    zu_recv,
    plane_send,
    plane_recv,
    x_send,
    x_recv,
):
    me = lax.axis_index("dp")
    z = lax.axis_index("tensor")
    opposite = lax.rem(z + RING // 2, RING)
    barrier = pltpu.get_barrier_semaphore()

    def greet(i, carry):
        pl.semaphore_signal(
            barrier,
            inc=1,
            device_id={"dp": lax.rem(me + i, OWNERS)},
            device_id_type=pl.DeviceIdType.MESH,
        )
        return carry

    lax.fori_loop(1, OWNERS, greet, 0)
    for steps in (1, RING // 2, RING - 1):
        pl.semaphore_signal(
            barrier,
            inc=1,
            device_id={"tensor": lax.rem(z + steps, RING)},
            device_id_type=pl.DeviceIdType.MESH,
        )

    last = pl.ds(OWN * BLK, BLK)
    loads = [
        pltpu.make_async_copy(teacher_hbm, teacher_ref, load_sem.at[6]),
        pltpu.make_async_copy(item_feats, item_rows.at[last], load_sem.at[0]),
        pltpu.make_async_copy(item_w_in, own_w.at[0], load_sem.at[1]),
        pltpu.make_async_copy(item_w_out, own_w.at[1], load_sem.at[2]),
        pltpu.make_async_copy(user_feats, user_rows.at[last], load_sem.at[3]),
        pltpu.make_async_copy(user_w_in, own_w.at[2], load_sem.at[4]),
        pltpu.make_async_copy(user_w_out, own_w.at[3], load_sem.at[5]),
    ]
    for load in loads:
        load.start()

    live = count_ref[0]

    def place(k, carry):
        pos_ref[k] = owner_ref[cand_ref[0, k]]
        return carry

    lax.fori_loop(0, SLOTS, place, 0)

    pl.semaphore_wait(barrier, OWNERS - 1 + 3)

    item_tower = Tower(
        item_rows, item_feats, hidden, item_partial, item_returned, items, (zi_send, zi_recv)
    )
    user_tower = Tower(
        user_rows, user_feats, hidden, user_partial, user_returned, users, (zu_send, zu_recv)
    )
    pieces = (
        (item_w, 0, 2 * SHARE),
        (user_w, 0, 2 * SHARE),
        (items, 0, BLK // 2),
        (items, BLK // 2, BLK // 2),
        (users, 0, BLK // 2),
        (users, BLK // 2, BLK // 2),
    )
    gathers = [
        PlaneGather(*piece, plane_send.at[n], plane_recv.at[n]) for n, piece in enumerate(pieces)
    ]
    user_gathers = gathers[4:]
    share = pl.ds(pl.multiple_of(me * SHARE, SHARE), SHARE)

    def shift(n):
        table = (item_w, item_w, user_w, user_w)[n]
        ref = (item_w_in, item_w_out, user_w_in, user_w_out)[n]
        return z_copy(
            ref.at[share],
            table.at[me, pl.ds((n % 2) * SHARE, SHARE)],
            shift_send.at[n],
            shift_recv.at[n],
            opposite,
        )

    def own_weights(n):
        return lambda cols: own_w[n, :, cols]

    def far_weights(table, part):
        def pick(cols):
            return table[:, pl.ds(part * SHARE, SHARE), cols].reshape(D, cols.size)

        return pick

    item_own = (own_weights(0), own_weights(1))
    user_own = (own_weights(2), own_weights(3))
    item_far = (far_weights(item_w, 0), far_weights(item_w, 1))
    user_far = (far_weights(user_w, 0), far_weights(user_w, 1))

    def shift_start(first):
        for n in (first, first + 1):
            shift(n).start()

    def weights_start(gather, first):
        for n in (first, first + 1):
            shift(n).wait_recv()
        gather.start()

    def own_slice(tower, weights, needed):
        for load in needed:
            load.wait()
        tower.features_here()
        tower.gemm(0, 4, *weights, False)

    def invert(j, carry):
        found = jnp.int32(SLOTS)
        for k in range(SLOTS):
            found = jnp.where((pos_ref[k] == j) & (k < live), k, found)
        inv_ref[j] = found
        return carry

    scale = 3.0 / math.sqrt(D)
    weight = BLK * SLOTS / 4.0 * scale

    def teacher_block(k):
        return teacher_ref[:, pl.ds(pl.multiple_of(k * BLK, BLK), BLK)]

    def usable(k, value, other):
        return jnp.where(k < live, value, other)

    def row_max(block):
        def step(k, high):
            return jnp.maximum(high, usable(k, block(k), -jnp.inf))

        high = lax.fori_loop(0, SLOTS, step, jnp.full((BLK, BLK), -jnp.inf, F32))
        return jnp.max(high, axis=1, keepdims=True)

    def row_sum(block, high):
        def step(k, total):
            return total + usable(k, jnp.exp(block(k) - high), 0.0)

        total = lax.fori_loop(0, SLOTS, step, jnp.zeros((BLK, BLK), F32))
        return jnp.sum(total, axis=1, keepdims=True)

    stats = {}

    def softmax_stats(name, block):
        high = row_max(block)
        total = row_sum(block, high)
        stats[name] = (high, total, jnp.log(total))

    def teacher_stats():
        loads[0].wait()
        softmax_stats("teacher", teacher_block)

    def logit_step(k, carry):
        picked = items[pos_ref[k]]
        logits[k] = scale * lax.dot_general(
            users[me], picked, (((1,), (1,)), ((), ())), preferred_element_type=F32
        )
        return carry

    def student_block(k):
        return logits[k]

    def gradients(part):
        teacher_high, teacher_sum, teacher_log = stats["teacher"]
        student_high, student_sum, student_log = stats["student"]

        def grad_step(k, total):
            t_shift = teacher_block(k) - teacher_high
            s_shift = student_block(k) - student_high
            p = jnp.exp(t_shift) / teacher_sum
            q = jnp.exp(s_shift) / student_sum
            gap = (t_shift - teacher_log) - (s_shift - student_log)
            g = usable(k, weight * (q - p), 0.0)
            grads[k] = g.astype(BF16)
            grads_t[k] = g.T.astype(BF16)
            return total + usable(k, p * gap, 0.0)

        before = jnp.zeros((BLK, BLK), F32) if part == 0 else diverged[...]
        half = SLOTS // 2
        diverged[...] = lax.fori_loop(half * part, half * part + half, grad_step, before)

    def exchange(slot, target):
        return dp_copy(
            g_send.at[target], g_recv.at[slot], x_send.at[target], x_recv.at[slot], target
        )

    def send_grads(i, carry):
        target = lax.rem(me + i, OWNERS)
        g_send[target] = grads_t[inv_ref[target]]
        exchange(me, target).start()
        return carry

    def all_to_all():
        grads_t[SLOTS] = jnp.zeros((BLK, BLK), BF16)
        lax.fori_loop(1, OWNERS, send_grads, 0)
        g_recv[me] = grads_t[inv_ref[me]]

    wide = 256

    def user_gradient():
        row_total = jnp.broadcast_to(jnp.sum(diverged[...], axis=1, keepdims=True), (BLK, BLK))
        out_ref[pl.ds(2 * BLK, 8), pl.ds(0, BLK)] = 0.5 * row_total.T[0:8, :]
        for chunk in range(D // wide):
            cols = pl.ds(chunk * wide, wide)

            def user_step(k, acc):
                picked = items[pos_ref[k], :, cols]
                return acc + jnp.dot(grads[k], picked, preferred_element_type=F32)

            zero = jnp.zeros((BLK, wide), F32)
            out_ref[pl.ds(0, BLK), cols] = 0.5 * lax.fori_loop(0, SLOTS, user_step, zero)

    def landed():
        def one(i, carry):
            source = lax.rem(me + OWNERS - i, OWNERS)
            dp_copy(
                g_send.at[source], g_recv.at[source], x_send.at[source], x_recv.at[source], me
            ).wait_recv()
            return carry

        lax.fori_loop(1, OWNERS, one, 0)

    written = []
    item_rows_out = pl.ds(BLK, BLK)

    def item_gradient(sources):
        def one(n, carry):
            cols = pl.ds(pl.multiple_of(n * wide, wide), wide)
            acc = out_ref[item_rows_out, cols] if first_done else jnp.zeros((BLK, wide), F32)
            for j in sources:
                contrib = jnp.dot(g_recv[j], users[j, :, cols], preferred_element_type=F32)
                acc = acc + 0.5 * contrib.astype(BF16).astype(F32)
            out_ref[item_rows_out, cols] = acc
            return carry

        first_done = bool(written)
        written.append(True)
        lax.fori_loop(0, D // wide, one, 0)

    def from_own(qb):
        item_gradient([gathers[4].index(OFF[q], OFF[qb]) for q in range(SIDE)])

    def from_other(qb):
        for gather in user_gathers:
            for qa in range(SIDE):
                gather.from_partner(qa, qb)
        item_gradient([gathers[4].partner_index(OFF[q], OFF[qb]) for q in range(SIDE)])

    part = functools.partial
    tasks = {
        "invert": lambda: lax.fori_loop(0, OWNERS, invert, 0),
        "tstat": teacher_stats,
        "sstat": part(softmax_stats, "student", student_block),
        "a2a": all_to_all,
        "ugrad": user_gradient,
        "landed": landed,
    }
    for name, gather in zip(("WI", "WU", "IT0", "IT1", "US0", "US1"), gathers):
        tasks.update(gather.tasks(name))
    towers = (
        ("_i", item_tower, item_own, item_far, loads[1:4], gathers[0]),
        ("_u", user_tower, user_own, user_far, loads[4:7], gathers[1]),
    )
    for n, (end, tower, own, far, needed, gather) in enumerate(towers):
        tasks["shift" + end] = part(shift_start, 2 * n)
        tasks[("WI.start", "WU.start")[n]] = part(weights_start, gather, 2 * n)
        tasks["feats" + end] = tower.send_features
        tasks["pass" + end] = tower.pass_features
        tasks["own" + end] = part(own_slice, tower, own, needed)
        for pair in range(2):
            tasks["far" + str(pair) + end] = part(tower.gemm, 2 * pair, 2, *far, True)
            tasks["pass" + str(pair) + end] = part(tower.pass_far, pair)
            tasks["finish" + str(pair) + end] = part(tower.finish, pair)
        tasks["sendfar" + end] = tower.send_far
        tasks["sendnear" + end] = tower.send_near
    for n in range(4):
        tasks["logit" + str(n)] = part(lax.fori_loop, 4 * n, 4 * n + 4, logit_step, 0)
        tasks["own" + str(n)] = part(from_own, n)
        tasks["oth" + str(n)] = part(from_other, n)
    for n in range(2):
        tasks["grad" + str(n)] = part(gradients, n)
    for name in ORDER:
        tasks[name]()

    for n in range(4):
        shift(n).wait_send()
    item_tower.drain()
    user_tower.drain()
    for gather in gathers:
        gather.drain()

    def drained(i, carry):
        target = lax.rem(me + i, OWNERS)
        exchange(me, target).wait_send()
        return carry

    lax.fori_loop(1, OWNERS, drained, 0)


def shards(
    user_feats,
    item_feats,
    user_w_in,
    user_w_out,
    item_w_in,
    item_w_out,
    teacher,
    cand_blocks,
    cand_count,
    owner_map,
):
    hbm = pl.BlockSpec(memory_space=pl.ANY)
    vmem = pl.BlockSpec(memory_space=pltpu.VMEM)
    smem = pl.BlockSpec(memory_space=pltpu.SMEM)
    dma = pltpu.SemaphoreType.DMA
    halves = pl.pallas_call(
        step_kernel,
        out_shape=jax.ShapeDtypeStruct((2 * BLK + 8, D), F32),
        in_specs=[hbm] * 7 + [smem] * 3,
        out_specs=vmem,
        scratch_shapes=[
            pltpu.VMEM((OWNERS, BLK, D), BF16),
            pltpu.VMEM((OWNERS, BLK, D), BF16),
            pltpu.VMEM((4, D, D), BF16),
            pltpu.VMEM((OWNERS, 2 * SHARE, D), BF16),
            pltpu.VMEM((OWNERS, 2 * SHARE, D), BF16),
            pltpu.VMEM((4 * BLK, D), BF16),
            pltpu.VMEM((4 * BLK, D), BF16),
            pltpu.VMEM((4 * BLK, D), BF16),
            pltpu.VMEM((4 * BLK, D), F32),
            pltpu.VMEM((4 * BLK, D), F32),
            pltpu.VMEM((3 * BLK, D), F32),
            pltpu.VMEM((3 * BLK, D), F32),
            pltpu.VMEM((BLK, SLOTS * BLK), F32),
            pltpu.VMEM((SLOTS, BLK, BLK), F32),
            pltpu.VMEM((BLK, BLK), F32),
            pltpu.VMEM((SLOTS, BLK, BLK), BF16),
            pltpu.VMEM((SLOTS + 1, BLK, BLK), BF16),
            pltpu.VMEM((OWNERS, BLK, BLK), BF16),
            pltpu.VMEM((OWNERS, BLK, BLK), BF16),
            pltpu.SMEM((SLOTS,), jnp.int32),
            pltpu.SMEM((OWNERS,), jnp.int32),
            dma((7,)),
            dma((4,)),
            dma((4,)),
            dma((9,)),
            dma((9,)),
            dma((9,)),
            dma((9,)),
            dma((6, 36)),
            dma((6, 36)),
            dma((OWNERS,)),
            dma((OWNERS,)),
        ],
        compiler_params=pltpu.CompilerParams(
            collective_id=0, has_side_effects=True, vmem_limit_bytes=62 * 1024 * 1024
        ),
        name="distill_step",
    )(
        user_feats,
        item_feats,
        user_w_in,
        user_w_out,
        item_w_in,
        item_w_out,
        teacher,
        cand_blocks,
        cand_count,
        owner_map,
    )
    return (2.0 * halves[2 * BLK, :BLK], 2.0 * halves[:BLK], 2.0 * halves[BLK : 2 * BLK])


def solution(mesh):
    placed = (
        P(("dp", "tensor"), None),
        P(("dp", "tensor"), None),
        P(None, "tensor"),
        P("tensor", None),
        P(None, "tensor"),
        P("tensor", None),
        P(("dp", "tensor"), None),
        P(("dp", "tensor"), None),
        P(("dp", "tensor")),
        P(),
    )
    return jax.shard_map(
        shards,
        mesh=mesh,
        in_specs=placed,
        out_specs=(P(("dp", "tensor")), P(("dp", "tensor"), None), P(("dp", "tensor"), None)),
        check_vma=False,
    )
```

```python
import functools
import math

import jax
import jax.numpy as jnp
from jax import lax
from jax.experimental import pallas as pl
from jax.experimental.pallas import tpu as pltpu
from jax.sharding import PartitionSpec as P

BLK = 128
D = 1024
SLOTS = 16
OWNERS = 32
SIDE = 4
OFF = (0, 3, 1, 2)
SHARE = BLK // SIDE
RING = 8
FAR2, FAR1, NEAR, OWN = range(4)
HALF = BLK // 2
F32 = jnp.float32
BF16 = jnp.bfloat16


def dp_copy(src, dst, send_sem, recv_sem, target):
    return pltpu.make_async_remote_copy(
        src_ref=src,
        dst_ref=dst,
        send_sem=send_sem,
        recv_sem=recv_sem,
        device_id={"dp": target},
        device_id_type=pl.DeviceIdType.MESH,
    )


def z_copy(src, dst, send_sem, recv_sem, target):
    return pltpu.make_async_remote_copy(
        src_ref=src,
        dst_ref=dst,
        send_sem=send_sem,
        recv_sem=recv_sem,
        device_id={"tensor": target},
        device_id_type=pl.DeviceIdType.MESH,
    )


ORDER = (
    "shift_i", "shift_u", "tstat", "invert", "WI.start", "feats_i", "WI.from_a0", "WI.from_a1", "WI.from_b00",
    "WI.from_b01", "WI.far_a", "WI.from_b10", "WI.from_b11", "WI.from_b20", "pass_i", "WI.from_b21",
    "WI.far_b0", "WI.from_b30", "WI.from_b31", "WU.start", "feats_u", "WI.far_b1", "WI.far_b2", "own_i",
    "WU.from_a0", "WU.from_a1", "WU.from_b00", "WU.from_b01", "WI.far_b3", "pass_u", "WI.partners", "far0_i",
    "send0_i", "WU.far_a", "WU.from_b10", "WU.from_b11", "WU.from_b20", "WU.from_b21", "far1_i", "send1_i",
    "WU.far_b0", "WU.from_b30", "WU.from_b31", "own_u", "pass0_i", "WU.far_b1", "WU.far_b2", "WU.far_b3",
    "WU.partners", "far0_u", "pass1_i", "finish0_i", "send0_u", "IT0.start", "far1_u", "send1_u", "finish1_i",
    "IT1.start", "IT0.from_a0", "IT0.from_a1", "IT0.from_b00", "IT0.from_b01", "IT1.from_a0", "IT1.from_a1",
    "IT1.from_b00", "IT1.from_b01", "pass0_u", "IT0.far_a", "IT0.from_b11", "IT0.from_b10", "IT1.far_a",
    "IT0.from_b20", "IT0.from_b21", "IT0.far_b0", "pass1_u", "IT1.from_b10", "IT1.from_b11", "IT1.from_b20",
    "IT1.from_b21", "finish0_u", "IT1.far_b0", "IT0.from_b30", "IT0.from_b31", "IT0.far_b1", "finish1_u",
    "IT1.from_b30", "IT1.from_b31", "US.start", "IT0.far_b2", "IT1.far_b1", "IT1.far_b2", "IT0.far_b3",
    "IT0.partners", "IT1.far_b3", "IT1.partners", "logit0", "logit1", "US.from_a0", "US.from_a1", "logit2",
    "US.from_b00", "US.from_b01", "logit3", "sstat", "grad0", "US.far_a", "US.from_b10", "US.from_b11",
    "grad1", "a2a", "US.from_b20", "US.from_b21", "ugrad", "US.far_b0", "US.from_b30", "US.from_b31",
    "US.far_b1", "US.far_b2", "US.far_b3", "landed", "own0", "oth0", "own1", "oth1", "own2", "oth2", "own3",
    "oth3",
)


class PlaneGather:
    def __init__(self, table, base, rows, send, recv):
        self.table, self.base, self.rows = table, base, rows
        self.send, self.recv = send, recv
        me = lax.axis_index("dp")
        core = lax.rem(me, 2)
        x, y = me // 8, lax.rem(me // 2, SIDE)
        self.me, self.core = me, core
        self.a = x + core * (y - x)
        self.b = y + core * (x - y)
        self.stride_a = SIDE - 3 * core
        self.stride_b = 1 + 3 * core
        self.pending = []

    def index(self, off_a, off_b):
        a = lax.rem(self.a + off_a, SIDE)
        b = lax.rem(self.b + off_b, SIDE)
        return (a * self.stride_a + b * self.stride_b) * 2 + self.core

    def partner_index(self, off_a, off_b):
        other = 1 - self.core
        a = lax.rem(self.b + off_a, SIDE)
        b = lax.rem(self.a + off_b, SIDE)
        return (a * self.stride_b + b * self.stride_a) * 2 + other

    def block(self, slot, half=None):
        if half is None:
            return self.table.at[slot, pl.ds(self.base, self.rows)]
        return self.table.at[slot, pl.ds(self.base + half * (self.rows // 2), self.rows // 2)]

    def go(self, ident, slot, target, half=None):
        ref = self.block(slot, half)
        copy = dp_copy(ref, ref, self.send.at[ident], self.recv.at[ident], target)
        copy.start()
        self.pending.append(copy)

    def arrived(self, ident, slot, half=None):
        ref = self.block(slot, half)
        dp_copy(ref, ref, self.send.at[ident], self.recv.at[ident], self.me).wait_recv()

    def to_partner(self, qa, qb):
        self.go(20 + 4 * qa + qb, self.index(OFF[qa], OFF[qb]), self.me + 1 - 2 * self.core)

    def along_b(self, q):
        slot = self.index(OFF[q], 0)
        self.go(4 + 2 * q, slot, self.index(0, 1))
        self.go(5 + 2 * q, slot, self.index(0, 3))

    def start(self):
        slot = self.index(0, 0)
        self.go(0, slot, self.index(1, 0))
        self.go(1, slot, self.index(3, 0))
        self.along_b(0)
        self.to_partner(0, 0)

    def from_a(self, side):
        q = 1 + side
        slot = self.index(OFF[q], 0)
        self.arrived(side, slot)
        self.go(2 + side, slot, self.index(1 if side == 0 else 3, 0), side)
        self.along_b(q)
        self.to_partner(q, 0)

    def far_a(self):
        slot = self.index(2, 0)
        self.arrived(2, slot, 0)
        self.arrived(3, slot, 1)
        self.along_b(3)
        self.to_partner(3, 0)

    def from_b(self, q, side):
        slot = self.index(OFF[q], OFF[1 + side])
        self.arrived(4 + 2 * q + side, slot)
        self.go(12 + 2 * q + side, slot, self.index(0, 1 if side == 0 else 3), side)
        self.to_partner(q, 1 + side)

    def far_b(self, q):
        slot = self.index(OFF[q], 2)
        self.arrived(12 + 2 * q, slot, 0)
        self.arrived(13 + 2 * q, slot, 1)
        self.to_partner(q, 3)

    def from_partner(self, qa, qb):
        self.arrived(20 + 4 * qa + qb, self.partner_index(OFF[qa], OFF[qb]))

    def drain(self):
        for copy in self.pending:
            copy.wait_send()

    def partners(self):
        for qa in range(SIDE):
            for qb in range(SIDE):
                self.from_partner(qa, qb)

    def tasks(self, name):
        table = {
            name + ".start": self.start,
            name + ".far_a": self.far_a,
            name + ".partners": self.partners,
        }
        for side in range(2):
            table[name + ".from_a" + str(side)] = functools.partial(self.from_a, side)
        for q in range(SIDE):
            table[name + ".far_b" + str(q)] = functools.partial(self.far_b, q)
            for side in range(2):
                label = name + ".from_b" + str(q) + str(side)
                table[label] = functools.partial(self.from_b, q, side)
        return table


class Tower:
    def __init__(self, feats, shard, hidden, partial, returned, table, sems):
        self.feats, self.shard, self.hidden = feats, shard, hidden
        self.partial, self.returned, self.table = partial, returned, table
        self.send, self.recv = sems
        self.z = lax.axis_index("tensor")
        self.me = lax.axis_index("dp")
        self.sign = 1 - 2 * lax.rem(self.me, 2)
        self.pending = []

    def at(self, steps):
        return lax.rem(self.z + steps * self.sign + RING, RING)

    def go(self, ident, src, dst, target):
        copy = z_copy(src, dst, self.send.at[ident], self.recv.at[ident], target)
        copy.start()
        self.pending.append(copy)

    def arrived(self, ident, dst):
        z_copy(dst, dst, self.send.at[ident], self.recv.at[ident], self.z).wait_recv()

    def send_features(self):
        for part in range(2):
            source = self.shard.at[pl.ds(part * HALF, HALF)]
            self.go(part, source, self.feats.at[part, FAR1], self.at(1))
            self.go(2 + part, source, self.feats.at[part, NEAR], self.at(-1))

    def pass_features(self):
        for part in range(2):
            here = self.feats.at[part, FAR1]
            self.arrived(part, here)
            self.go(4 + part, here, self.feats.at[part, FAR2], self.at(1))

    def features_here(self):
        for part in range(2):
            self.arrived(2 + part, self.feats.at[part, NEAR])
            self.arrived(4 + part, self.feats.at[part, FAR2])

    def gemm(self, first, count, w_in, w_out, more):
        rows = count * 4 * HALF
        parts = pl.ds(first, count)
        held = pl.ds(0, rows)
        wide = 256

        def into_hidden(n, carry):
            cols = pl.ds(pl.multiple_of(n * wide, wide), wide)
            feats = self.feats[parts].reshape(rows, D)
            out = jnp.dot(feats, w_in(cols), preferred_element_type=F32)
            self.hidden[held, cols] = jnp.maximum(out, 0.0).astype(BF16)
            return carry

        def into_partial(n, carry):
            cols = pl.ds(pl.multiple_of(n * wide, wide), wide)
            out = jnp.dot(self.hidden[held, :], w_out(cols), preferred_element_type=F32)
            out = out.reshape(count, 4, HALF, wide)
            if more:
                out = out + self.partial[parts, :, :, cols]
            self.partial[parts, :, :, cols] = out
            return carry

        lax.fori_loop(0, D // wide, into_hidden, 0)
        lax.fori_loop(0, D // wide, into_partial, 0)

    def send_partial(self, part):
        self.go(6 + part, self.partial.at[part, FAR2], self.returned.at[part, 0], self.at(-1))
        self.go(8 + part, self.partial.at[part, NEAR], self.returned.at[part, 2], self.at(1))

    def pass_far(self, part):
        self.arrived(6 + part, self.returned.at[part, 0])
        self.partial[part, FAR1] = self.partial[part, FAR1] + self.returned[part, 0]
        self.go(10 + part, self.partial.at[part, FAR1], self.returned.at[part, 1], self.at(-1))

    def finish(self, part):
        self.arrived(10 + part, self.returned.at[part, 1])
        self.arrived(8 + part, self.returned.at[part, 2])
        total = self.partial[part, OWN] + self.returned[part, 1] + self.returned[part, 2]
        self.table[self.me, pl.ds(part * HALF, HALF), :] = total.astype(BF16)

    def drain(self):
        for copy in self.pending:
            copy.wait_send()


def step_kernel(
    user_feats,
    item_feats,
    user_w_in,
    user_w_out,
    item_w_in,
    item_w_out,
    teacher_hbm,
    cand_ref,
    count_ref,
    owner_ref,
    out_ref,
    items,
    users,
    own_w,
    item_w,
    user_w,
    item_rows,
    user_rows,
    hidden,
    item_partial,
    user_partial,
    item_returned,
    user_returned,
    teacher_ref,
    logits,
    diverged,
    grads,
    grads_t,
    g_send,
    g_recv,
    pos_ref,
    inv_ref,
    load_sem,
    shift_send,
    shift_recv,
    zi_send,
    zi_recv,
    zu_send,
    zu_recv,
    plane_send,
    plane_recv,
    x_send,
    x_recv,
):
    me = lax.axis_index("dp")
    z = lax.axis_index("tensor")
    opposite = lax.rem(z + RING // 2, RING)
    barrier = pltpu.get_barrier_semaphore()

    def greet(i, carry):
        pl.semaphore_signal(
            barrier,
            inc=1,
            device_id={"dp": lax.rem(me + i, OWNERS)},
            device_id_type=pl.DeviceIdType.MESH,
        )
        return carry

    lax.fori_loop(1, OWNERS, greet, 0)
    for steps in (1, RING // 2, RING - 1):
        pl.semaphore_signal(
            barrier,
            inc=1,
            device_id={"tensor": lax.rem(z + steps, RING)},
            device_id_type=pl.DeviceIdType.MESH,
        )

    upper, lower = pl.ds(0, HALF), pl.ds(HALF, HALF)
    loads = [
        pltpu.make_async_copy(teacher_hbm, teacher_ref, load_sem.at[6]),
        pltpu.make_async_copy(item_feats.at[upper], item_rows.at[0, OWN], load_sem.at[0]),
        pltpu.make_async_copy(item_feats.at[lower], item_rows.at[1, OWN], load_sem.at[7]),
        pltpu.make_async_copy(item_w_in, own_w.at[0], load_sem.at[1]),
        pltpu.make_async_copy(item_w_out, own_w.at[1], load_sem.at[2]),
        pltpu.make_async_copy(user_feats.at[upper], user_rows.at[0, OWN], load_sem.at[3]),
        pltpu.make_async_copy(user_feats.at[lower], user_rows.at[1, OWN], load_sem.at[8]),
        pltpu.make_async_copy(user_w_in, own_w.at[2], load_sem.at[4]),
        pltpu.make_async_copy(user_w_out, own_w.at[3], load_sem.at[5]),
    ]
    for load in loads:
        load.start()

    live = count_ref[0]

    def place(k, carry):
        pos_ref[k] = owner_ref[cand_ref[0, k]]
        return carry

    lax.fori_loop(0, SLOTS, place, 0)

    pl.semaphore_wait(barrier, OWNERS - 1 + 3)

    item_tower = Tower(
        item_rows, item_feats, hidden, item_partial, item_returned, items, (zi_send, zi_recv)
    )
    user_tower = Tower(
        user_rows, user_feats, hidden, user_partial, user_returned, users, (zu_send, zu_recv)
    )
    pieces = (
        (item_w, 0, 2 * SHARE),
        (user_w, 0, 2 * SHARE),
        (items, 0, BLK // 2),
        (items, BLK // 2, BLK // 2),
        (users, 0, BLK),
    )
    gathers = [
        PlaneGather(*piece, plane_send.at[n], plane_recv.at[n]) for n, piece in enumerate(pieces)
    ]
    user_gather = gathers[4]
    share = pl.ds(pl.multiple_of(me * SHARE, SHARE), SHARE)

    def shift(n):
        table = (item_w, item_w, user_w, user_w)[n]
        ref = (item_w_in, item_w_out, user_w_in, user_w_out)[n]
        return z_copy(
            ref.at[share],
            table.at[me, pl.ds((n % 2) * SHARE, SHARE)],
            shift_send.at[n],
            shift_recv.at[n],
            opposite,
        )

    def own_weights(n):
        return lambda cols: own_w[n, :, cols]

    def far_weights(table, part):
        def pick(cols):
            return table[:, pl.ds(part * SHARE, SHARE), cols].reshape(D, cols.size)

        return pick

    item_own = (own_weights(0), own_weights(1))
    user_own = (own_weights(2), own_weights(3))
    item_far = (far_weights(item_w, 0), far_weights(item_w, 1))
    user_far = (far_weights(user_w, 0), far_weights(user_w, 1))

    def shift_start(first):
        for n in (first, first + 1):
            shift(n).start()

    def weights_start(gather, first):
        for n in (first, first + 1):
            shift(n).wait_recv()
        gather.start()

    def own_slice(tower, weights, needed):
        for load in needed:
            load.wait()
        tower.features_here()
        tower.gemm(0, 2, *weights, False)

    def invert(j, carry):
        found = jnp.int32(SLOTS)
        for k in range(SLOTS):
            found = jnp.where((pos_ref[k] == j) & (k < live), k, found)
        inv_ref[j] = found
        return carry

    scale = 3.0 / math.sqrt(D)
    weight = BLK * SLOTS / 4.0 * scale

    def teacher_block(k):
        return teacher_ref[:, pl.ds(pl.multiple_of(k * BLK, BLK), BLK)]

    def usable(k, value, other):
        return jnp.where(k < live, value, other)

    def row_max(block):
        def step(k, high):
            return jnp.maximum(high, usable(k, block(k), -jnp.inf))

        high = lax.fori_loop(0, SLOTS, step, jnp.full((BLK, BLK), -jnp.inf, F32))
        return jnp.max(high, axis=1, keepdims=True)

    def row_sum(block, high):
        def step(k, total):
            return total + usable(k, jnp.exp(block(k) - high), 0.0)

        total = lax.fori_loop(0, SLOTS, step, jnp.zeros((BLK, BLK), F32))
        return jnp.sum(total, axis=1, keepdims=True)

    stats = {}

    def softmax_stats(name, block):
        high = row_max(block)
        total = row_sum(block, high)
        stats[name] = (high, total, jnp.log(total))

    def teacher_stats():
        loads[0].wait()
        softmax_stats("teacher", teacher_block)

    def logit_step(k, carry):
        picked = items[pos_ref[k]]
        logits[k] = scale * lax.dot_general(
            users[me], picked, (((1,), (1,)), ((), ())), preferred_element_type=F32
        )
        return carry

    def student_block(k):
        return logits[k]

    def gradients(part):
        teacher_high, teacher_sum, teacher_log = stats["teacher"]
        student_high, student_sum, student_log = stats["student"]

        def grad_step(k, total):
            t_shift = teacher_block(k) - teacher_high
            s_shift = student_block(k) - student_high
            p = jnp.exp(t_shift) / teacher_sum
            q = jnp.exp(s_shift) / student_sum
            gap = (t_shift - teacher_log) - (s_shift - student_log)
            g = usable(k, weight * (q - p), 0.0)
            grads[k] = g.astype(BF16)
            grads_t[k] = g.T.astype(BF16)
            return total + usable(k, p * gap, 0.0)

        before = jnp.zeros((BLK, BLK), F32) if part == 0 else diverged[...]
        half = SLOTS // 2
        diverged[...] = lax.fori_loop(half * part, half * part + half, grad_step, before)

    def exchange(slot, target):
        return dp_copy(
            g_send.at[target], g_recv.at[slot], x_send.at[target], x_recv.at[slot], target
        )

    def send_grads(i, carry):
        target = lax.rem(me + i, OWNERS)
        g_send[target] = grads_t[inv_ref[target]]
        exchange(me, target).start()
        return carry

    def all_to_all():
        grads_t[SLOTS] = jnp.zeros((BLK, BLK), BF16)
        lax.fori_loop(1, OWNERS, send_grads, 0)
        g_recv[me] = grads_t[inv_ref[me]]

    wide = 256

    def user_gradient():
        row_total = jnp.broadcast_to(jnp.sum(diverged[...], axis=1, keepdims=True), (BLK, BLK))
        out_ref[pl.ds(2 * BLK, 8), pl.ds(0, BLK)] = 0.5 * row_total.T[0:8, :]
        for chunk in range(D // wide):
            cols = pl.ds(chunk * wide, wide)

            def user_step(k, acc):
                picked = items[pos_ref[k], :, cols]
                return acc + jnp.dot(grads[k], picked, preferred_element_type=F32)

            zero = jnp.zeros((BLK, wide), F32)
            out_ref[pl.ds(0, BLK), cols] = 0.5 * lax.fori_loop(0, SLOTS, user_step, zero)

    def landed():
        def one(i, carry):
            source = lax.rem(me + OWNERS - i, OWNERS)
            dp_copy(
                g_send.at[source], g_recv.at[source], x_send.at[source], x_recv.at[source], me
            ).wait_recv()
            return carry

        lax.fori_loop(1, OWNERS, one, 0)

    written = []
    item_rows_out = pl.ds(BLK, BLK)

    def item_gradient(sources):
        def one(n, carry):
            cols = pl.ds(pl.multiple_of(n * wide, wide), wide)
            acc = out_ref[item_rows_out, cols] if first_done else jnp.zeros((BLK, wide), F32)
            for j in sources:
                contrib = jnp.dot(g_recv[j], users[j, :, cols], preferred_element_type=F32)
                acc = acc + 0.5 * contrib.astype(BF16).astype(F32)
            out_ref[item_rows_out, cols] = acc
            return carry

        first_done = bool(written)
        written.append(True)
        lax.fori_loop(0, D // wide, one, 0)

    def from_own(qb):
        item_gradient([user_gather.index(OFF[q], OFF[qb]) for q in range(SIDE)])

    def from_other(qb):
        for qa in range(SIDE):
            user_gather.from_partner(qa, qb)
        item_gradient([user_gather.partner_index(OFF[q], OFF[qb]) for q in range(SIDE)])

    part = functools.partial
    tasks = {
        "invert": lambda: lax.fori_loop(0, OWNERS, invert, 0),
        "tstat": teacher_stats,
        "sstat": part(softmax_stats, "student", student_block),
        "a2a": all_to_all,
        "ugrad": user_gradient,
        "landed": landed,
    }
    for name, gather in zip(("WI", "WU", "IT0", "IT1", "US"), gathers):
        tasks.update(gather.tasks(name))
    towers = (
        ("_i", item_tower, item_own, item_far, loads[1:5], gathers[0]),
        ("_u", user_tower, user_own, user_far, loads[5:9], gathers[1]),
    )
    for n, (end, tower, own, far, needed, gather) in enumerate(towers):
        tasks["shift" + end] = part(shift_start, 2 * n)
        tasks[("WI.start", "WU.start")[n]] = part(weights_start, gather, 2 * n)
        tasks["feats" + end] = tower.send_features
        tasks["pass" + end] = tower.pass_features
        tasks["own" + end] = part(own_slice, tower, own, needed)
        for pair in range(2):
            tasks["far" + str(pair) + end] = part(tower.gemm, pair, 1, *far, True)
            tasks["send" + str(pair) + end] = part(tower.send_partial, pair)
            tasks["pass" + str(pair) + end] = part(tower.pass_far, pair)
            tasks["finish" + str(pair) + end] = part(tower.finish, pair)
    for n in range(4):
        tasks["logit" + str(n)] = part(lax.fori_loop, 4 * n, 4 * n + 4, logit_step, 0)
        tasks["own" + str(n)] = part(from_own, n)
        tasks["oth" + str(n)] = part(from_other, n)
    for n in range(2):
        tasks["grad" + str(n)] = part(gradients, n)
    for name in ORDER:
        tasks[name]()

    for n in range(4):
        shift(n).wait_send()
    item_tower.drain()
    user_tower.drain()
    for gather in gathers:
        gather.drain()

    def drained(i, carry):
        target = lax.rem(me + i, OWNERS)
        exchange(me, target).wait_send()
        return carry

    lax.fori_loop(1, OWNERS, drained, 0)


def shards(
    user_feats,
    item_feats,
    user_w_in,
    user_w_out,
    item_w_in,
    item_w_out,
    teacher,
    cand_blocks,
    cand_count,
    owner_map,
):
    hbm = pl.BlockSpec(memory_space=pl.ANY)
    vmem = pl.BlockSpec(memory_space=pltpu.VMEM)
    smem = pl.BlockSpec(memory_space=pltpu.SMEM)
    dma = pltpu.SemaphoreType.DMA
    halves = pl.pallas_call(
        step_kernel,
        out_shape=jax.ShapeDtypeStruct((2 * BLK + 8, D), F32),
        in_specs=[hbm] * 7 + [smem] * 3,
        out_specs=vmem,
        scratch_shapes=[
            pltpu.VMEM((OWNERS, BLK, D), BF16),
            pltpu.VMEM((OWNERS, BLK, D), BF16),
            pltpu.VMEM((4, D, D), BF16),
            pltpu.VMEM((OWNERS, 2 * SHARE, D), BF16),
            pltpu.VMEM((OWNERS, 2 * SHARE, D), BF16),
            pltpu.VMEM((2, 4, HALF, D), BF16),
            pltpu.VMEM((2, 4, HALF, D), BF16),
            pltpu.VMEM((4 * BLK, D), BF16),
            pltpu.VMEM((2, 4, HALF, D), F32),
            pltpu.VMEM((2, 4, HALF, D), F32),
            pltpu.VMEM((2, 3, HALF, D), F32),
            pltpu.VMEM((2, 3, HALF, D), F32),
            pltpu.VMEM((BLK, SLOTS * BLK), F32),
            pltpu.VMEM((SLOTS, BLK, BLK), F32),
            pltpu.VMEM((BLK, BLK), F32),
            pltpu.VMEM((SLOTS, BLK, BLK), BF16),
            pltpu.VMEM((SLOTS + 1, BLK, BLK), BF16),
            pltpu.VMEM((OWNERS, BLK, BLK), BF16),
            pltpu.VMEM((OWNERS, BLK, BLK), BF16),
            pltpu.SMEM((SLOTS,), jnp.int32),
            pltpu.SMEM((OWNERS,), jnp.int32),
            dma((9,)),
            dma((4,)),
            dma((4,)),
            dma((12,)),
            dma((12,)),
            dma((12,)),
            dma((12,)),
            dma((5, 36)),
            dma((5, 36)),
            dma((OWNERS,)),
            dma((OWNERS,)),
        ],
        compiler_params=pltpu.CompilerParams(
            collective_id=0, has_side_effects=True, vmem_limit_bytes=62 * 1024 * 1024
        ),
        name="distill_step",
    )(
        user_feats,
        item_feats,
        user_w_in,
        user_w_out,
        item_w_in,
        item_w_out,
        teacher,
        cand_blocks,
        cand_count,
        owner_map,
    )
    return (2.0 * halves[2 * BLK, :BLK], 2.0 * halves[:BLK], 2.0 * halves[BLK : 2 * BLK])


def solution(mesh):
    placed = (
        P(("dp", "tensor"), None),
        P(("dp", "tensor"), None),
        P(None, "tensor"),
        P("tensor", None),
        P(None, "tensor"),
        P("tensor", None),
        P(("dp", "tensor"), None),
        P(("dp", "tensor"), None),
        P(("dp", "tensor")),
        P(),
    )
    return jax.shard_map(
        shards,
        mesh=mesh,
        in_specs=placed,
        out_specs=(P(("dp", "tensor")), P(("dp", "tensor"), None), P(("dp", "tensor"), None)),
        check_vma=False,
    )
```

```python
import functools
import math

import jax
import jax.numpy as jnp
from jax import lax
from jax.experimental import pallas as pl
from jax.experimental.pallas import tpu as pltpu
from jax.sharding import PartitionSpec as P

BLK = 128
D = 1024
SLOTS = 16
OWNERS = 32
SIDE = 4
OFF = (0, 3, 1, 2)
SHARE = BLK // SIDE
RING = 8
FAR2, FAR1, NEAR, OWN = range(4)
HALF = BLK // 2
F32 = jnp.float32
BF16 = jnp.bfloat16


def dp_copy(src, dst, send_sem, recv_sem, target):
    return pltpu.make_async_remote_copy(
        src_ref=src,
        dst_ref=dst,
        send_sem=send_sem,
        recv_sem=recv_sem,
        device_id={"dp": target},
        device_id_type=pl.DeviceIdType.MESH,
    )


def z_copy(src, dst, send_sem, recv_sem, target):
    return pltpu.make_async_remote_copy(
        src_ref=src,
        dst_ref=dst,
        send_sem=send_sem,
        recv_sem=recv_sem,
        device_id={"tensor": target},
        device_id_type=pl.DeviceIdType.MESH,
    )


ORDER = (
    "shift_i", "shift_u", "tstat", "invert", "WI.start", "feats_i", "WI.from_a0", "WI.from_a1", "WI.from_b00",
    "WI.from_b01", "WI.far_a", "WI.from_b10", "WI.from_b11", "WI.from_b20", "pass_i", "WI.from_b21",
    "WI.far_b0", "WI.from_b30", "WI.from_b31", "WU.start", "feats_u", "WI.far_b1", "WI.far_b2", "own_i",
    "WU.from_a0", "WU.from_a1", "WU.from_b00", "WU.from_b01", "WI.far_b3", "pass_u", "WI.partners", "far0_i",
    "send0_i", "WU.far_a", "WU.from_b10", "WU.from_b11", "WU.from_b20", "WU.from_b21", "far1_i", "send1_i",
    "WU.far_b0", "WU.from_b30", "WU.from_b31", "pass0_i", "pass1_i", "own_u", "WU.far_b1", "WU.far_b2",
    "WU.far_b3", "WU.partners", "finish0_i", "IT0.start", "far0_u", "send0_u", "finish1_i", "IT1.start",
    "far1_u", "send1_u", "IT0.from_a0", "IT0.from_a1", "IT0.from_b00", "IT0.from_b01", "IT1.from_a0", "IT1.from_a1",
    "IT1.from_b00", "IT1.from_b01", "pass0_u", "IT0.far_a", "IT0.from_b11", "IT0.from_b10", "IT1.far_a",
    "IT0.from_b20", "IT0.from_b21", "IT0.far_b0", "pass1_u", "IT1.from_b10", "IT1.from_b11", "IT1.from_b20",
    "IT1.from_b21", "finish0_u", "IT1.far_b0", "IT0.from_b30", "IT0.from_b31", "IT0.far_b1", "finish1_u",
    "IT1.from_b30", "IT1.from_b31", "US.start", "IT0.far_b2", "IT1.far_b1", "IT1.far_b2", "IT0.far_b3",
    "IT0.partners", "IT1.far_b3", "IT1.partners", "logit0", "logit1", "US.from_a0", "US.from_a1", "logit2",
    "US.from_b00", "US.from_b01", "logit3", "sstat", "grad0", "US.far_a", "US.from_b10", "US.from_b11",
    "grad1", "a2a", "US.from_b20", "US.from_b21", "ugrad", "US.far_b0", "US.from_b30", "US.from_b31",
    "US.far_b1", "US.far_b2", "US.far_b3", "landed", "own0", "oth0", "own1", "oth1", "own2", "oth2", "own3",
    "oth3",
)


class PlaneGather:
    def __init__(self, table, base, rows, send, recv):
        self.table, self.base, self.rows = table, base, rows
        self.send, self.recv = send, recv
        me = lax.axis_index("dp")
        core = lax.rem(me, 2)
        x, y = me // 8, lax.rem(me // 2, SIDE)
        self.me, self.core = me, core
        self.a = x + core * (y - x)
        self.b = y + core * (x - y)
        self.stride_a = SIDE - 3 * core
        self.stride_b = 1 + 3 * core
        self.pending = []

    def index(self, off_a, off_b):
        a = lax.rem(self.a + off_a, SIDE)
        b = lax.rem(self.b + off_b, SIDE)
        return (a * self.stride_a + b * self.stride_b) * 2 + self.core

    def partner_index(self, off_a, off_b):
        other = 1 - self.core
        a = lax.rem(self.b + off_a, SIDE)
        b = lax.rem(self.a + off_b, SIDE)
        return (a * self.stride_b + b * self.stride_a) * 2 + other

    def block(self, slot, half=None):
        if half is None:
            return self.table.at[slot, pl.ds(self.base, self.rows)]
        return self.table.at[slot, pl.ds(self.base + half * (self.rows // 2), self.rows // 2)]

    def go(self, ident, slot, target, half=None):
        ref = self.block(slot, half)
        copy = dp_copy(ref, ref, self.send.at[ident], self.recv.at[ident], target)
        copy.start()
        self.pending.append(copy)

    def arrived(self, ident, slot, half=None):
        ref = self.block(slot, half)
        dp_copy(ref, ref, self.send.at[ident], self.recv.at[ident], self.me).wait_recv()

    def to_partner(self, qa, qb):
        self.go(20 + 4 * qa + qb, self.index(OFF[qa], OFF[qb]), self.me + 1 - 2 * self.core)

    def along_b(self, q):
        slot = self.index(OFF[q], 0)
        self.go(4 + 2 * q, slot, self.index(0, 1))
        self.go(5 + 2 * q, slot, self.index(0, 3))

    def start(self):
        slot = self.index(0, 0)
        self.go(0, slot, self.index(1, 0))
        self.go(1, slot, self.index(3, 0))
        self.along_b(0)
        self.to_partner(0, 0)

    def from_a(self, side):
        q = 1 + side
        slot = self.index(OFF[q], 0)
        self.arrived(side, slot)
        self.go(2 + side, slot, self.index(1 if side == 0 else 3, 0), side)
        self.along_b(q)
        self.to_partner(q, 0)

    def far_a(self):
        slot = self.index(2, 0)
        self.arrived(2, slot, 0)
        self.arrived(3, slot, 1)
        self.along_b(3)
        self.to_partner(3, 0)

    def from_b(self, q, side):
        slot = self.index(OFF[q], OFF[1 + side])
        self.arrived(4 + 2 * q + side, slot)
        self.go(12 + 2 * q + side, slot, self.index(0, 1 if side == 0 else 3), side)
        self.to_partner(q, 1 + side)

    def far_b(self, q):
        slot = self.index(OFF[q], 2)
        self.arrived(12 + 2 * q, slot, 0)
        self.arrived(13 + 2 * q, slot, 1)
        self.to_partner(q, 3)

    def from_partner(self, qa, qb):
        self.arrived(20 + 4 * qa + qb, self.partner_index(OFF[qa], OFF[qb]))

    def drain(self):
        for copy in self.pending:
            copy.wait_send()

    def partners(self):
        for qa in range(SIDE):
            for qb in range(SIDE):
                self.from_partner(qa, qb)

    def tasks(self, name):
        table = {
            name + ".start": self.start,
            name + ".far_a": self.far_a,
            name + ".partners": self.partners,
        }
        for side in range(2):
            table[name + ".from_a" + str(side)] = functools.partial(self.from_a, side)
        for q in range(SIDE):
            table[name + ".far_b" + str(q)] = functools.partial(self.far_b, q)
            for side in range(2):
                label = name + ".from_b" + str(q) + str(side)
                table[label] = functools.partial(self.from_b, q, side)
        return table


class Tower:
    def __init__(self, feats, shard, hidden, partial, returned, table, sems):
        self.feats, self.shard, self.hidden = feats, shard, hidden
        self.partial, self.returned, self.table = partial, returned, table
        self.send, self.recv = sems
        self.z = lax.axis_index("tensor")
        self.me = lax.axis_index("dp")
        self.sign = 1 - 2 * lax.rem(self.me, 2)
        self.pending = []

    def at(self, steps):
        return lax.rem(self.z + steps * self.sign + RING, RING)

    def go(self, ident, src, dst, target):
        copy = z_copy(src, dst, self.send.at[ident], self.recv.at[ident], target)
        copy.start()
        self.pending.append(copy)

    def arrived(self, ident, dst):
        z_copy(dst, dst, self.send.at[ident], self.recv.at[ident], self.z).wait_recv()

    def send_features(self):
        for part in range(2):
            source = self.shard.at[pl.ds(part * HALF, HALF)]
            self.go(part, source, self.feats.at[part, FAR1], self.at(1))
            self.go(2 + part, source, self.feats.at[part, NEAR], self.at(-1))

    def pass_features(self):
        for part in range(2):
            here = self.feats.at[part, FAR1]
            self.arrived(part, here)
            self.go(4 + part, here, self.feats.at[part, FAR2], self.at(1))

    def features_here(self):
        for part in range(2):
            self.arrived(2 + part, self.feats.at[part, NEAR])
            self.arrived(4 + part, self.feats.at[part, FAR2])

    def gemm(self, first, count, w_in, w_out, more):
        rows = count * 4 * HALF
        parts = pl.ds(first, count)
        held = pl.ds(0, rows)
        wide = 256

        def into_hidden(n, carry):
            cols = pl.ds(pl.multiple_of(n * wide, wide), wide)
            feats = self.feats[parts].reshape(rows, D)
            out = jnp.dot(feats, w_in(cols), preferred_element_type=F32)
            self.hidden[held, cols] = jnp.maximum(out, 0.0).astype(BF16)
            return carry

        def into_partial(n, carry):
            cols = pl.ds(pl.multiple_of(n * wide, wide), wide)
            out = jnp.dot(self.hidden[held, :], w_out(cols), preferred_element_type=F32)
            out = out.reshape(count, 4, HALF, wide)
            if more:
                out = out + self.partial[parts, :, :, cols]
            self.partial[parts, :, :, cols] = out
            return carry

        lax.fori_loop(0, D // wide, into_hidden, 0)
        lax.fori_loop(0, D // wide, into_partial, 0)

    def send_partial(self, part):
        self.go(6 + part, self.partial.at[part, FAR2], self.returned.at[part, 0], self.at(-1))
        self.go(8 + part, self.partial.at[part, NEAR], self.returned.at[part, 2], self.at(1))

    def pass_far(self, part):
        self.arrived(6 + part, self.returned.at[part, 0])
        self.partial[part, FAR1] = self.partial[part, FAR1] + self.returned[part, 0]
        self.go(10 + part, self.partial.at[part, FAR1], self.returned.at[part, 1], self.at(-1))

    def finish(self, part):
        self.arrived(10 + part, self.returned.at[part, 1])
        self.arrived(8 + part, self.returned.at[part, 2])
        total = self.partial[part, OWN] + self.returned[part, 1] + self.returned[part, 2]
        self.table[self.me, pl.ds(part * HALF, HALF), :] = total.astype(BF16)

    def drain(self):
        for copy in self.pending:
            copy.wait_send()


def step_kernel(
    user_feats,
    item_feats,
    user_w_in,
    user_w_out,
    item_w_in,
    item_w_out,
    teacher_hbm,
    cand_ref,
    count_ref,
    owner_ref,
    out_ref,
    items,
    users,
    own_w,
    item_w,
    user_w,
    item_rows,
    user_rows,
    hidden,
    item_partial,
    user_partial,
    item_returned,
    user_returned,
    teacher_ref,
    logits,
    diverged,
    grads,
    grads_t,
    g_send,
    g_recv,
    pos_ref,
    inv_ref,
    load_sem,
    shift_send,
    shift_recv,
    zi_send,
    zi_recv,
    zu_send,
    zu_recv,
    plane_send,
    plane_recv,
    x_send,
    x_recv,
):
    me = lax.axis_index("dp")
    z = lax.axis_index("tensor")
    opposite = lax.rem(z + RING // 2, RING)
    barrier = pltpu.get_barrier_semaphore()

    def greet(i, carry):
        pl.semaphore_signal(
            barrier,
            inc=1,
            device_id={"dp": lax.rem(me + i, OWNERS)},
            device_id_type=pl.DeviceIdType.MESH,
        )
        return carry

    lax.fori_loop(1, OWNERS, greet, 0)
    for steps in (1, RING // 2, RING - 1):
        pl.semaphore_signal(
            barrier,
            inc=1,
            device_id={"tensor": lax.rem(z + steps, RING)},
            device_id_type=pl.DeviceIdType.MESH,
        )

    upper, lower = pl.ds(0, HALF), pl.ds(HALF, HALF)
    loads = [
        pltpu.make_async_copy(teacher_hbm, teacher_ref, load_sem.at[6]),
        pltpu.make_async_copy(item_feats.at[upper], item_rows.at[0, OWN], load_sem.at[0]),
        pltpu.make_async_copy(item_feats.at[lower], item_rows.at[1, OWN], load_sem.at[7]),
        pltpu.make_async_copy(item_w_in, own_w.at[0], load_sem.at[1]),
        pltpu.make_async_copy(item_w_out, own_w.at[1], load_sem.at[2]),
        pltpu.make_async_copy(user_feats.at[upper], user_rows.at[0, OWN], load_sem.at[3]),
        pltpu.make_async_copy(user_feats.at[lower], user_rows.at[1, OWN], load_sem.at[8]),
        pltpu.make_async_copy(user_w_in, own_w.at[2], load_sem.at[4]),
        pltpu.make_async_copy(user_w_out, own_w.at[3], load_sem.at[5]),
    ]
    for load in loads:
        load.start()

    live = count_ref[0]

    def place(k, carry):
        pos_ref[k] = owner_ref[cand_ref[0, k]]
        return carry

    lax.fori_loop(0, SLOTS, place, 0)

    pl.semaphore_wait(barrier, OWNERS - 1 + 3)

    item_tower = Tower(
        item_rows, item_feats, hidden, item_partial, item_returned, items, (zi_send, zi_recv)
    )
    user_tower = Tower(
        user_rows, user_feats, hidden, user_partial, user_returned, users, (zu_send, zu_recv)
    )
    pieces = (
        (item_w, 0, 2 * SHARE),
        (user_w, 0, 2 * SHARE),
        (items, 0, BLK // 2),
        (items, BLK // 2, BLK // 2),
        (users, 0, BLK),
    )
    gathers = [
        PlaneGather(*piece, plane_send.at[n], plane_recv.at[n]) for n, piece in enumerate(pieces)
    ]
    user_gather = gathers[4]
    share = pl.ds(pl.multiple_of(me * SHARE, SHARE), SHARE)

    def shift(n):
        table = (item_w, item_w, user_w, user_w)[n]
        ref = (item_w_in, item_w_out, user_w_in, user_w_out)[n]
        return z_copy(
            ref.at[share],
            table.at[me, pl.ds((n % 2) * SHARE, SHARE)],
            shift_send.at[n],
            shift_recv.at[n],
            opposite,
        )

    def own_weights(n):
        return lambda cols: own_w[n, :, cols]

    def far_weights(table, part):
        def pick(cols):
            return table[:, pl.ds(part * SHARE, SHARE), cols].reshape(D, cols.size)

        return pick

    item_own = (own_weights(0), own_weights(1))
    user_own = (own_weights(2), own_weights(3))
    item_far = (far_weights(item_w, 0), far_weights(item_w, 1))
    user_far = (far_weights(user_w, 0), far_weights(user_w, 1))

    def shift_start(first):
        for n in (first, first + 1):
            shift(n).start()

    def weights_start(gather, first):
        for n in (first, first + 1):
            shift(n).wait_recv()
        gather.start()

    def own_slice(tower, weights, needed):
        for load in needed:
            load.wait()
        tower.features_here()
        tower.gemm(0, 2, *weights, False)

    def invert(j, carry):
        found = jnp.int32(SLOTS)
        for k in range(SLOTS):
            found = jnp.where((pos_ref[k] == j) & (k < live), k, found)
        inv_ref[j] = found
        return carry

    scale = 3.0 / math.sqrt(D)
    weight = BLK * SLOTS / 4.0 * scale

    def teacher_block(k):
        return teacher_ref[:, pl.ds(pl.multiple_of(k * BLK, BLK), BLK)]

    def usable(k, value, other):
        return jnp.where(k < live, value, other)

    def row_max(block):
        def step(k, high):
            return jnp.maximum(high, usable(k, block(k), -jnp.inf))

        high = lax.fori_loop(0, SLOTS, step, jnp.full((BLK, BLK), -jnp.inf, F32))
        return jnp.max(high, axis=1, keepdims=True)

    def row_sum(block, high):
        def step(k, total):
            return total + usable(k, jnp.exp(block(k) - high), 0.0)

        total = lax.fori_loop(0, SLOTS, step, jnp.zeros((BLK, BLK), F32))
        return jnp.sum(total, axis=1, keepdims=True)

    stats = {}

    def softmax_stats(name, block):
        high = row_max(block)
        total = row_sum(block, high)
        stats[name] = (high, total, jnp.log(total))

    def teacher_stats():
        loads[0].wait()
        softmax_stats("teacher", teacher_block)

    def logit_step(k, carry):
        picked = items[pos_ref[k]]
        logits[k] = scale * lax.dot_general(
            users[me], picked, (((1,), (1,)), ((), ())), preferred_element_type=F32
        )
        return carry

    def student_block(k):
        return logits[k]

    def gradients(part):
        teacher_high, teacher_sum, teacher_log = stats["teacher"]
        student_high, student_sum, student_log = stats["student"]

        def grad_step(k, total):
            t_shift = teacher_block(k) - teacher_high
            s_shift = student_block(k) - student_high
            p = jnp.exp(t_shift) / teacher_sum
            q = jnp.exp(s_shift) / student_sum
            gap = (t_shift - teacher_log) - (s_shift - student_log)
            g = usable(k, weight * (q - p), 0.0)
            grads[k] = g.astype(BF16)
            grads_t[k] = g.T.astype(BF16)
            return total + usable(k, p * gap, 0.0)

        before = jnp.zeros((BLK, BLK), F32) if part == 0 else diverged[...]
        half = SLOTS // 2
        diverged[...] = lax.fori_loop(half * part, half * part + half, grad_step, before)

    def exchange(slot, target):
        return dp_copy(
            g_send.at[target], g_recv.at[slot], x_send.at[target], x_recv.at[slot], target
        )

    def send_grads(i, carry):
        target = lax.rem(me + i, OWNERS)
        g_send[target] = grads_t[inv_ref[target]]
        exchange(me, target).start()
        return carry

    def all_to_all():
        grads_t[SLOTS] = jnp.zeros((BLK, BLK), BF16)
        lax.fori_loop(1, OWNERS, send_grads, 0)
        g_recv[me] = grads_t[inv_ref[me]]

    wide = 256

    def user_gradient():
        row_total = jnp.broadcast_to(jnp.sum(diverged[...], axis=1, keepdims=True), (BLK, BLK))
        out_ref[pl.ds(2 * BLK, 8), pl.ds(0, BLK)] = 0.5 * row_total.T[0:8, :]
        for chunk in range(D // wide):
            cols = pl.ds(chunk * wide, wide)

            def user_step(k, acc):
                picked = items[pos_ref[k], :, cols]
                return acc + jnp.dot(grads[k], picked, preferred_element_type=F32)

            zero = jnp.zeros((BLK, wide), F32)
            out_ref[pl.ds(0, BLK), cols] = 0.5 * lax.fori_loop(0, SLOTS, user_step, zero)

    def landed():
        def one(i, carry):
            source = lax.rem(me + OWNERS - i, OWNERS)
            dp_copy(
                g_send.at[source], g_recv.at[source], x_send.at[source], x_recv.at[source], me
            ).wait_recv()
            return carry

        lax.fori_loop(1, OWNERS, one, 0)

    written = []
    item_rows_out = pl.ds(BLK, BLK)

    def item_gradient(sources):
        def one(n, carry):
            cols = pl.ds(pl.multiple_of(n * wide, wide), wide)
            acc = out_ref[item_rows_out, cols] if first_done else jnp.zeros((BLK, wide), F32)
            for j in sources:
                contrib = jnp.dot(g_recv[j], users[j, :, cols], preferred_element_type=F32)
                acc = acc + 0.5 * contrib.astype(BF16).astype(F32)
            out_ref[item_rows_out, cols] = acc
            return carry

        first_done = bool(written)
        written.append(True)
        lax.fori_loop(0, D // wide, one, 0)

    def from_own(qb):
        item_gradient([user_gather.index(OFF[q], OFF[qb]) for q in range(SIDE)])

    def from_other(qb):
        for qa in range(SIDE):
            user_gather.from_partner(qa, qb)
        item_gradient([user_gather.partner_index(OFF[q], OFF[qb]) for q in range(SIDE)])

    part = functools.partial
    tasks = {
        "invert": lambda: lax.fori_loop(0, OWNERS, invert, 0),
        "tstat": teacher_stats,
        "sstat": part(softmax_stats, "student", student_block),
        "a2a": all_to_all,
        "ugrad": user_gradient,
        "landed": landed,
    }
    for name, gather in zip(("WI", "WU", "IT0", "IT1", "US"), gathers):
        tasks.update(gather.tasks(name))
    towers = (
        ("_i", item_tower, item_own, item_far, loads[1:5], gathers[0]),
        ("_u", user_tower, user_own, user_far, loads[5:9], gathers[1]),
    )
    for n, (end, tower, own, far, needed, gather) in enumerate(towers):
        tasks["shift" + end] = part(shift_start, 2 * n)
        tasks[("WI.start", "WU.start")[n]] = part(weights_start, gather, 2 * n)
        tasks["feats" + end] = tower.send_features
        tasks["pass" + end] = tower.pass_features
        tasks["own" + end] = part(own_slice, tower, own, needed)
        for pair in range(2):
            tasks["far" + str(pair) + end] = part(tower.gemm, pair, 1, *far, True)
            tasks["send" + str(pair) + end] = part(tower.send_partial, pair)
            tasks["pass" + str(pair) + end] = part(tower.pass_far, pair)
            tasks["finish" + str(pair) + end] = part(tower.finish, pair)
    for n in range(4):
        tasks["logit" + str(n)] = part(lax.fori_loop, 4 * n, 4 * n + 4, logit_step, 0)
        tasks["own" + str(n)] = part(from_own, n)
        tasks["oth" + str(n)] = part(from_other, n)
    for n in range(2):
        tasks["grad" + str(n)] = part(gradients, n)
    for name in ORDER:
        tasks[name]()

    for n in range(4):
        shift(n).wait_send()
    item_tower.drain()
    user_tower.drain()
    for gather in gathers:
        gather.drain()

    def drained(i, carry):
        target = lax.rem(me + i, OWNERS)
        exchange(me, target).wait_send()
        return carry

    lax.fori_loop(1, OWNERS, drained, 0)


def shards(
    user_feats,
    item_feats,
    user_w_in,
    user_w_out,
    item_w_in,
    item_w_out,
    teacher,
    cand_blocks,
    cand_count,
    owner_map,
):
    hbm = pl.BlockSpec(memory_space=pl.ANY)
    vmem = pl.BlockSpec(memory_space=pltpu.VMEM)
    smem = pl.BlockSpec(memory_space=pltpu.SMEM)
    dma = pltpu.SemaphoreType.DMA
    halves = pl.pallas_call(
        step_kernel,
        out_shape=jax.ShapeDtypeStruct((2 * BLK + 8, D), F32),
        in_specs=[hbm] * 7 + [smem] * 3,
        out_specs=vmem,
        scratch_shapes=[
            pltpu.VMEM((OWNERS, BLK, D), BF16),
            pltpu.VMEM((OWNERS, BLK, D), BF16),
            pltpu.VMEM((4, D, D), BF16),
            pltpu.VMEM((OWNERS, 2 * SHARE, D), BF16),
            pltpu.VMEM((OWNERS, 2 * SHARE, D), BF16),
            pltpu.VMEM((2, 4, HALF, D), BF16),
            pltpu.VMEM((2, 4, HALF, D), BF16),
            pltpu.VMEM((4 * BLK, D), BF16),
            pltpu.VMEM((2, 4, HALF, D), F32),
            pltpu.VMEM((2, 4, HALF, D), F32),
            pltpu.VMEM((2, 3, HALF, D), F32),
            pltpu.VMEM((2, 3, HALF, D), F32),
            pltpu.VMEM((BLK, SLOTS * BLK), F32),
            pltpu.VMEM((SLOTS, BLK, BLK), F32),
            pltpu.VMEM((BLK, BLK), F32),
            pltpu.VMEM((SLOTS, BLK, BLK), BF16),
            pltpu.VMEM((SLOTS + 1, BLK, BLK), BF16),
            pltpu.VMEM((OWNERS, BLK, BLK), BF16),
            pltpu.VMEM((OWNERS, BLK, BLK), BF16),
            pltpu.SMEM((SLOTS,), jnp.int32),
            pltpu.SMEM((OWNERS,), jnp.int32),
            dma((9,)),
            dma((4,)),
            dma((4,)),
            dma((12,)),
            dma((12,)),
            dma((12,)),
            dma((12,)),
            dma((5, 36)),
            dma((5, 36)),
            dma((OWNERS,)),
            dma((OWNERS,)),
        ],
        compiler_params=pltpu.CompilerParams(
            collective_id=0, has_side_effects=True, vmem_limit_bytes=62 * 1024 * 1024
        ),
        name="distill_step",
    )(
        user_feats,
        item_feats,
        user_w_in,
        user_w_out,
        item_w_in,
        item_w_out,
        teacher,
        cand_blocks,
        cand_count,
        owner_map,
    )
    return (2.0 * halves[2 * BLK, :BLK], 2.0 * halves[:BLK], 2.0 * halves[BLK : 2 * BLK])


def solution(mesh):
    placed = (
        P(("dp", "tensor"), None),
        P(("dp", "tensor"), None),
        P(None, "tensor"),
        P("tensor", None),
        P(None, "tensor"),
        P("tensor", None),
        P(("dp", "tensor"), None),
        P(("dp", "tensor"), None),
        P(("dp", "tensor")),
        P(),
    )
    return jax.shard_map(
        shards,
        mesh=mesh,
        in_specs=placed,
        out_specs=(P(("dp", "tensor")), P(("dp", "tensor"), None), P(("dp", "tensor"), None)),
        check_vma=False,
    )
```
